32 devices in a mesh: clip: 2 (over x), seq: 16 (over z, y, core).
Axes of the slice: x: 2, y: 2, z: 4, core: 2. Of those that a mesh axis runs over, the one named last changes fastest.
Arguments:
- video_query: bfloat16 [512, 4096], P(('clip', 'seq')), parts along dimension 0, may hold values from -6 to 6
- video_keys: bfloat16 [512, 4096], P(('clip', 'seq')), parts along dimension 0, may hold values from -6 to 6
- video_values: bfloat16 [512, 4096], P(('clip', 'seq')), parts along dimension 0, may hold values from -6 to 6
- audio_query: bfloat16 [256, 2048], P(('clip', 'seq')), parts along dimension 0, may hold values from -6 to 6
- audio_keys: bfloat16 [256, 2048], P(('clip', 'seq')), parts along dimension 0, may hold values from -6 to 6
- audio_values: bfloat16 [256, 2048], P(('clip', 'seq')), parts along dimension 0, may hold values from -6 to 6
- cross_video_query: bfloat16 [512, 2048], P(('clip', 'seq')), parts along dimension 0, may hold values from -6 to 6
- cross_video_keys: bfloat16 [512, 2048], P(('clip', 'seq')), parts along dimension 0, may hold values from -6 to 6
- cross_video_values: bfloat16 [512, 2048], P(('clip', 'seq')), parts along dimension 0, may hold values from -6 to 6
- cross_audio_query: bfloat16 [256, 2048], P(('clip', 'seq')), parts along dimension 0, may hold values from -6 to 6
- cross_audio_keys: bfloat16 [256, 2048], P(('clip', 'seq')), parts along dimension 0, may hold values from -6 to 6
- cross_audio_values: bfloat16 [256, 2048], P(('clip', 'seq')), parts along dimension 0, may hold values from -6 to 6
- video_length: int32 [2], P('clip'), parts along dimension 0, may hold values from 128 to 256
- audio_length: int32 [2], P('clip'), parts along dimension 0, may hold values from 64 to 128
- align_offset: int32 [2], P('clip'), parts along dimension 0, may hold values from -8 to 8
Outputs:
- video_mixed: bfloat16 [512, 4096], P(('clip', 'seq')), parts along dimension 0
- audio_mixed: bfloat16 [256, 2048], P(('clip', 'seq')), parts along dimension 0
- video_cross: bfloat16 [512, 2048], P(('clip', 'seq')), parts along dimension 0
- audio_cross: bfloat16 [256, 2048], P(('clip', 'seq')), parts along dimension 0
The draws below stay inside these ranges and needn't reach their ends.
There are 2 independent parts, one for each index of `clip`. The reference program is written for one: setup_inputs(seed, part) draws one part's arguments, and reference() takes and returns one part's arrays. A program takes and returns all parts, laid end to end along the dimension named above; each array names one. Nothing has to cross between parts.
All inputs are finite; a program needn't handle non-finite values.
Results may differ from the reference program's by a relative error of at most 0.006.
Values may be sent and summed in bfloat16 or wider, within the bound.
A program may use at most 128 MiB of HBM per device.

```python
import math
import jax
import jax.numpy as jnp
from jax import lax

HV = 32
HDV = 128
HA = 32
HDA = 64
DV = 4096
DA = 2048
TV = 256
TA = 128
AWIN = 80
VWIN = 32


def base_field(key, rows, width):
    values = jnp.clip(jax.random.normal(key, (rows, width), dtype=jnp.float32), -6.0, 6.0)
    return values


def plant_queries(values, key):
    return values.astype(jnp.bfloat16)


def plant_keys(values, key):
    return values.astype(jnp.bfloat16)


def draw_video_query(key, part):
    return plant_queries(base_field(jax.random.fold_in(key, 101), TV, DV), key)


def draw_video_keys(key, part):
    return plant_keys(base_field(jax.random.fold_in(key, 102), TV, DV), key)


def draw_audio_query(key, part):
    return plant_queries(base_field(jax.random.fold_in(key, 103), TA, DA), key)


def draw_audio_keys(key, part):
    return plant_keys(base_field(jax.random.fold_in(key, 104), TA, DA), key)


def draw_cross_video_query(key, part):
    return plant_queries(base_field(jax.random.fold_in(key, 105), TV, DA), key)


def draw_cross_audio_keys(key, part):
    return plant_keys(base_field(jax.random.fold_in(key, 106), TA, DA), key)


def draw_cross_audio_query(key, part):
    return plant_queries(base_field(jax.random.fold_in(key, 107), TA, DA), key)


def draw_cross_video_keys(key, part):
    return plant_keys(base_field(jax.random.fold_in(key, 108), TV, DA), key)


def level_of(key, extent, pieces, least, largest):
    def one(axis_at, parts):
        heights = jax.random.uniform(jax.random.fold_in(jax.random.fold_in(key, 6), axis_at), (parts,), jnp.float32, least / len(pieces), largest / len(pieces))
        return jnp.repeat(jnp.exp(heights), extent[axis_at] // parts).reshape((-1,) + (1,) * (len(extent) - axis_at - 1))

    factor_of = one(*pieces[0])
    for cut in pieces[1:]:
        factor_of = factor_of * one(*cut)
    return factor_of


def gaussian(rng, shape, scale, reach, shards=(), kind=jnp.bfloat16):
    level = level_of(rng, shape, shards, -0.22, 0.18) if shards else 1.0
    values = jax.random.normal(rng, shape, jnp.float32) * scale * level
    return jnp.minimum(jnp.maximum(values, -reach), reach).astype(kind)


def setup_inputs(seed: int = 0, part: int = 0) -> dict:
    splits = jax.random.split(jax.random.key(seed), 16)
    part_splits = jax.random.split(jax.random.fold_in(splits[15], part), 16)
    return {
        "video_query": draw_video_query(jax.random.fold_in(jax.random.fold_in(splits[15], part), 71), part),
        "video_keys": draw_video_keys(jax.random.fold_in(jax.random.fold_in(splits[15], part), 71), part),
        "video_values": gaussian(part_splits[2], (TV, DV), 1.0, 6.0, ((0, 16),)),
        "audio_query": draw_audio_query(jax.random.fold_in(jax.random.fold_in(splits[15], part), 71), part),
        "audio_keys": draw_audio_keys(jax.random.fold_in(jax.random.fold_in(splits[15], part), 71), part),
        "audio_values": gaussian(part_splits[5], (TA, DA), 1.0, 6.0, ((0, 16),)),
        "cross_video_query": draw_cross_video_query(jax.random.fold_in(jax.random.fold_in(splits[15], part), 71), part),
        "cross_video_keys": draw_cross_video_keys(jax.random.fold_in(jax.random.fold_in(splits[15], part), 71), part),
        "cross_video_values": gaussian(part_splits[8], (TV, DA), 1.0, 6.0, ((0, 16),)),
        "cross_audio_query": draw_cross_audio_query(jax.random.fold_in(jax.random.fold_in(splits[15], part), 71), part),
        "cross_audio_keys": draw_cross_audio_keys(jax.random.fold_in(jax.random.fold_in(splits[15], part), 71), part),
        "cross_audio_values": gaussian(part_splits[11], (TA, DA), 1.0, 6.0, ((0, 16),)),
        "video_length": jax.random.randint(part_splits[12], (1,), TV // 2, TV + 1).astype(jnp.int32),
        "audio_length": jax.random.randint(part_splits[13], (1,), TA // 2, TA + 1).astype(jnp.int32),
        "align_offset": jax.random.randint(part_splits[14], (1,), -(TA // 16), TA // 16 + 1).astype(jnp.int32),
    }


def block_size(total, limit):
    chosen = min(total, limit)
    while total % chosen:
        chosen -= 1
    return chosen

def exact_attention(queries, keys, values, heads, depth, query_pos, key_pos, allowed):
    count = queries.shape[0]
    key_count = keys.shape[0]
    head_queries = queries.reshape(count, heads, depth).transpose(1, 0, 2)
    head_keys = keys.reshape(key_count, heads, depth).transpose(1, 0, 2)
    head_values = values.reshape(key_count, heads, depth).transpose(1, 0, 2)
    q_block = block_size(count, 512)
    scale = 1.0 / math.sqrt(depth)
    places = query_pos.reshape(count // q_block, q_block)

    def one_head(packed):
        one_query, one_key, one_value = packed
        tiles = one_query.reshape(count // q_block, q_block, depth)

        def one_tile(tile_pack):
            tile, tile_pos = tile_pack
            scores = jnp.dot(tile, one_key.T, preferred_element_type=jnp.float32) * scale
            permit = allowed(tile_pos[:, None], key_pos[None, :])
            scores = jnp.where(permit, scores, -jnp.inf)
            peak = lax.optimization_barrier(jnp.max(scores, axis=1, keepdims=True))
            weights = jnp.exp(scores - peak)
            total = lax.optimization_barrier(jnp.sum(weights, axis=1, keepdims=True))
            mixed = jnp.dot(weights.astype(jnp.bfloat16), one_value, preferred_element_type=jnp.float32)
            return (mixed / total).astype(jnp.bfloat16)
        return lax.map(one_tile, (tiles, places)).reshape(count, depth)
    result = lax.map(one_head, (head_queries, head_keys, head_values))
    return result.transpose(1, 0, 2).reshape(count, heads * depth)

def reference(video_query, video_keys, video_values, audio_query, audio_keys, audio_values, cross_video_query, cross_video_keys, cross_video_values, cross_audio_query, cross_audio_keys, cross_audio_values, video_length, audio_length, align_offset):
    video_valid = video_length[0]
    audio_valid = audio_length[0]
    align_shift = align_offset[0]
    video_places = jnp.arange(TV, dtype=jnp.int32)
    audio_places = jnp.arange(TA, dtype=jnp.int32)

    def video_open(q_where, k_where):
        return k_where < video_valid

    def audio_open(q_where, k_where):
        return k_where < audio_valid

    def toward_video(q_where, k_where):
        center = jnp.clip(q_where * TA // TV + align_shift, 0, audio_valid - 1)
        return (k_where < audio_valid) & (jnp.abs(k_where - center) <= AWIN)

    def toward_audio(q_where, k_where):
        center = jnp.clip((q_where - align_shift) * TV // TA, 0, video_valid - 1)
        return (k_where < video_valid) & (jnp.abs(k_where - center) <= VWIN)
    video_mixed = exact_attention(video_query, video_keys, video_values, HV, HDV, video_places, video_places, video_open)
    audio_mixed = exact_attention(audio_query, audio_keys, audio_values, HA, HDA, audio_places, audio_places, audio_open)
    video_cross = exact_attention(cross_video_query, cross_audio_keys, cross_audio_values, HA, HDA, video_places, audio_places, toward_video)
    audio_cross = exact_attention(cross_audio_query, cross_video_keys, cross_video_values, HA, HDA, audio_places, video_places, toward_audio)
    return (video_mixed, audio_mixed, video_cross, audio_cross)
```

```python
import functools
import math

import jax
import jax.numpy as jnp
from jax import lax
from jax.experimental import pallas as pl
from jax.experimental.pallas import tpu as pltpu
from jax.sharding import PartitionSpec as P

HV = 32
HDV = 128
HA = 32
HDA = 64


def block_size(total, limit):
    chosen = min(total, limit)
    while total % chosen:
        chosen -= 1
    return chosen


def split_heads(tokens, heads, depth, copies):
    rows = tokens.shape[0]
    shaped = tokens.reshape(copies, rows // copies, heads, depth).transpose(2, 0, 1, 3)
    return shaped.reshape(heads * copies, rows // copies, depth)


def spread_heads(tokens, heads, depth, copies):
    rows = tokens.shape[0]
    shaped = tokens.reshape(rows, heads, depth).transpose(1, 0, 2)
    shaped = jnp.broadcast_to(shaped[:, None], (heads, copies, rows, depth))
    return shaped.reshape(heads * copies, rows, depth)


def join_heads(owned, heads, depth, copies):
    part_rows = owned.shape[1]
    shaped = owned.reshape(heads, copies, part_rows, depth).transpose(1, 2, 0, 3)
    return shaped.reshape(copies * part_rows, heads * depth)


def owned_positions(rows, copies, devices, index):
    part_rows = rows // copies
    flat = jnp.arange(devices * part_rows, dtype=jnp.int32)
    return flat // part_rows * rows + index % copies * part_rows + flat % part_rows


def online_update(carry, scores, permit, value_tile, value_form):
    running, total, accum = carry
    scores = jnp.where(permit, scores, -1e30)
    newmax = jnp.maximum(running, jnp.max(scores, axis=2))
    weights = jnp.where(permit, jnp.exp(scores - newmax[:, :, None]), 0.0)
    factor = jnp.exp(running - newmax)
    total = total * factor + jnp.sum(weights, axis=2)
    mixed = jnp.einsum(
        value_form, weights.astype(jnp.bfloat16), value_tile, preferred_element_type=jnp.float32
    )
    accum = accum * factor[:, :, None] + mixed
    return (newmax, total, accum)


def fold_initial(rows, heads, depth):
    return (
        jnp.full((heads, rows), -1e30, jnp.float32),
        jnp.zeros((heads, rows), jnp.float32),
        jnp.zeros((heads, rows, depth), jnp.float32),
    )


def fold_piece(carry, local_query, key_rows, value_rows, permit, heads, depth):
    keyed = key_rows.reshape(key_rows.shape[0], heads, depth)
    valued = value_rows.reshape(value_rows.shape[0], heads, depth)
    scores = jnp.einsum("qhd,khd->hqk", local_query, keyed, preferred_element_type=jnp.float32) * (
        1.0 / math.sqrt(depth)
    )
    return online_update(carry, scores, permit[None], valued, "hqk,khd->hqd")


def fold_finish(carry, heads, depth):
    running, total, accum = carry
    result = (accum / total[:, :, None]).astype(jnp.bfloat16)
    return result.transpose(1, 0, 2).reshape(result.shape[1], heads * depth)


def attend_local(queries, keys, values, query_pos, key_pos, allowed):
    heads, q_count, depth = queries.shape
    k_count = keys.shape[1]
    q_block = block_size(q_count, 512)
    k_block = block_size(k_count, 2048)
    scale = 1.0 / math.sqrt(depth)
    q_tiles = queries.reshape(heads, q_count // q_block, q_block, depth).transpose(1, 0, 2, 3)
    k_tiles = keys.reshape(heads, k_count // k_block, k_block, depth).transpose(1, 0, 2, 3)
    v_tiles = values.reshape(heads, k_count // k_block, k_block, depth).transpose(1, 0, 2, 3)
    q_places = query_pos.reshape(q_count // q_block, q_block)
    k_places = key_pos.reshape(k_count // k_block, k_block)

    def one_tile(packed):
        q_tile, q_where = packed

        def absorb(carry, piece):
            k_tile, v_tile, k_where = piece
            scores = (
                jnp.einsum("hqd,hkd->hqk", q_tile, k_tile, preferred_element_type=jnp.float32)
                * scale
            )
            permit = allowed(q_where[:, None], k_where[None, :])[None]
            return (online_update(carry, scores, permit, v_tile, "hqk,hkd->hqd"), None)

        initial = fold_initial(q_block, heads, depth)
        final_state, unused = lax.scan(absorb, initial, (k_tiles, v_tiles, k_places))
        running, total, accum = final_state
        return (accum / total[:, :, None]).astype(jnp.bfloat16)

    tiles = lax.map(one_tile, (q_tiles, q_places))
    return tiles.transpose(1, 0, 2, 3).reshape(heads, q_count, depth)


def shards(
    video_query,
    video_keys,
    video_values,
    audio_query,
    audio_keys,
    audio_values,
    cross_video_query,
    cross_video_keys,
    cross_video_values,
    cross_audio_query,
    cross_audio_keys,
    cross_audio_values,
    video_length,
    audio_length,
    align_offset,
):
    devices = lax.axis_size("seq")
    index = lax.axis_index("seq")
    video_rows = video_query.shape[0]
    audio_rows = audio_query.shape[0]
    video_total = video_rows * devices
    audio_total = audio_rows * devices
    video_reach = video_total // 8
    audio_reach = 5 * audio_total // 8
    video_valid = video_length[0]
    audio_valid = audio_length[0]
    align_shift = align_offset[0]
    copies = max(devices // HV, 1)
    video_places = jnp.arange(video_total, dtype=jnp.int32)
    audio_places = jnp.arange(audio_total, dtype=jnp.int32)

    def video_open(q_where, k_where):
        return k_where < video_valid

    def toward_video(q_where, k_where):
        center = jnp.clip(q_where * audio_total // video_total + align_shift, 0, audio_valid - 1)
        return (k_where < audio_valid) & (jnp.abs(k_where - center) <= audio_reach)

    def toward_audio(q_where, k_where):
        center = jnp.clip((q_where - align_shift) * video_total // audio_total, 0, video_valid - 1)
        return (k_where < video_valid) & (jnp.abs(k_where - center) <= video_reach)

    video_owned = (
        lax.all_to_all(
            split_heads(video_query, HV, HDV, copies),
            "seq",
            split_axis=0,
            concat_axis=1,
            tiled=True,
        ),
        lax.all_to_all(
            spread_heads(video_keys, HV, HDV, copies),
            "seq",
            split_axis=0,
            concat_axis=1,
            tiled=True,
        ),
        lax.all_to_all(
            spread_heads(video_values, HV, HDV, copies),
            "seq",
            split_axis=0,
            concat_axis=1,
            tiled=True,
        ),
    )
    video_done = attend_local(
        video_owned[0],
        video_owned[1],
        video_owned[2],
        owned_positions(video_rows, copies, devices, index),
        video_places,
        video_open,
    )
    video_mixed = join_heads(
        lax.all_to_all(video_done, "seq", split_axis=1, concat_axis=0, tiled=True), HV, HDV, copies
    )
    audio_local = audio_query.reshape(audio_rows, HA, HDA)
    piece = (
        lax.all_gather(audio_keys, "seq", axis=0, tiled=True),
        lax.all_gather(audio_values, "seq", axis=0, tiled=True),
    )
    k_where = jnp.arange(piece[0].shape[0], dtype=jnp.int32)
    audio_k_where = k_where[None, :]
    permit = audio_k_where < audio_valid
    audio_state = fold_piece(
        fold_initial(audio_rows, HA, HDA), audio_local, piece[0], piece[1], permit, HA, HDA
    )
    audio_mixed = fold_finish(audio_state, HA, HDA)
    cross_owned = (
        lax.all_to_all(
            split_heads(cross_video_query, HA, HDA, copies),
            "seq",
            split_axis=0,
            concat_axis=1,
            tiled=True,
        ),
        lax.all_to_all(
            spread_heads(cross_audio_keys, HA, HDA, copies),
            "seq",
            split_axis=0,
            concat_axis=1,
            tiled=True,
        ),
        lax.all_to_all(
            spread_heads(cross_audio_values, HA, HDA, copies),
            "seq",
            split_axis=0,
            concat_axis=1,
            tiled=True,
        ),
    )
    cross_done = attend_local(
        cross_owned[0],
        cross_owned[1],
        cross_owned[2],
        owned_positions(video_rows, copies, devices, index),
        audio_places,
        toward_video,
    )
    video_cross = join_heads(
        lax.all_to_all(cross_done, "seq", split_axis=1, concat_axis=0, tiled=True), HA, HDA, copies
    )
    listen_owned = (
        lax.all_to_all(
            split_heads(cross_audio_query, HA, HDA, copies),
            "seq",
            split_axis=0,
            concat_axis=1,
            tiled=True,
        ),
        lax.all_to_all(
            spread_heads(cross_video_keys, HA, HDA, copies),
            "seq",
            split_axis=0,
            concat_axis=1,
            tiled=True,
        ),
        lax.all_to_all(
            spread_heads(cross_video_values, HA, HDA, copies),
            "seq",
            split_axis=0,
            concat_axis=1,
            tiled=True,
        ),
    )
    listen_done = attend_local(
        listen_owned[0],
        listen_owned[1],
        listen_owned[2],
        owned_positions(audio_rows, copies, devices, index),
        video_places,
        toward_audio,
    )
    audio_cross = join_heads(
        lax.all_to_all(listen_done, "seq", split_axis=1, concat_axis=0, tiled=True), HA, HDA, copies
    )
    return (video_mixed, audio_mixed, video_cross, audio_cross)


LANES = 128

GROUPS = (
    ((0, 1, 2), 0, False),
    ((3, 4, 5), 1, False),
    ((6, 10, 11), 2, True),
    ((9, 7, 8), 3, True),
)


def softmax_mix(query, keys, values, permit, scale):
    scores = lax.dot_general(
        query, keys, (((1,), (1,)), ((), ())), preferred_element_type=jnp.float32
    )
    scores = jnp.where(permit, scores * scale, -1e30)
    peak = jnp.max(scores, axis=1, keepdims=True)
    weights = jnp.exp(scores - peak)
    total = jnp.sum(weights, axis=1, keepdims=True)
    mixed = jnp.dot(weights.astype(jnp.bfloat16), values, preferred_element_type=jnp.float32)
    return mixed / total


def read_tokens(ref, column):
    block = ref[:, :, column : column + LANES]
    n, rows, _ = block.shape
    if rows % 16:
        return block.astype(jnp.float32).reshape(n * rows, LANES).astype(block.dtype)
    return block.reshape(n * rows, LANES)


def write_tokens(ref, column, result):
    n, rows, _ = ref.shape
    ref[:, :, column : column + LANES] = result.reshape(n, rows, LANES).astype(ref.dtype)


def margin_blocks(n, video_rows):
    return min(-(-(3 * n * video_rows // 16) // video_rows), n // 2)


def held_shapes(n, arrays):
    half = n // 2
    shapes = [None] * 12
    for group, which, halved in GROUPS:
        for place, at in enumerate(group):
            rows, cols = arrays[at].shape
            blocks = n
            if halved and place == 0:
                blocks = half
            elif which == 3:
                blocks = half + margin_blocks(n, rows)
            shapes[at] = (blocks, rows, cols // (half if halved else n))
    return shapes


def fused_kernel(n, ratio, *refs):
    video_length, audio_length, align_offset = refs[:3]
    arrays = refs[3:15]
    outs = refs[15:19]
    held = refs[19:31]
    results = refs[31:35]
    send_sem, far_sem, recv_sem, back_send, back_recv, stage_sem = refs[35:]
    half = n // 2
    quarter = n // 4
    margin = held[7].shape[0] - half
    me = lax.axis_index("seq")
    side = me // half
    inner = lax.rem(me, half)
    near = (me >= half - margin) & (me < half + margin)

    def columns(width, owner):
        return pl.ds(pl.multiple_of(owner * width, LANES), width)

    def slot_of(group, which, halved, at, to_side):
        if halved and at == group[0]:
            return inner
        if which == 3:
            return me - to_side * (half - margin)
        return me

    def send(at, owner, slot, peer, sem):
        pltpu.make_async_remote_copy(
            src_ref=arrays[at].at[:, columns(held[at].shape[2], owner)],
            dst_ref=held[at].at[slot],
            send_sem=sem.at[at],
            recv_sem=recv_sem.at[at],
            device_id={"seq": peer},
            device_id_type=pl.DeviceIdType.MESH,
        ).start()

    for group, which, halved in GROUPS:
        for at in group:
            pltpu.make_async_copy(
                arrays[at].at[:, columns(held[at].shape[2], inner if halved else me)],
                held[at].at[slot_of(group, which, halved, at, side)],
                recv_sem.at[at],
            ).start()

    level = me // quarter
    rank = lax.rem(me, quarter)
    central = (level == 1) | (level == 2)
    here = level * quarter
    sibling = (level + 1 - 2 * lax.rem(level, 2)) * quarter
    far_center = (2 - side) * quarter
    far_edge = (3 - 3 * side) * quarter

    barrier = pltpu.get_barrier_semaphore()

    def signal(sem, peer):
        pl.semaphore_signal(
            sem, inc=1, device_id={"seq": peer}, device_id_type=pl.DeviceIdType.MESH
        )

    @pl.loop(1, quarter)
    def _(step):
        signal(barrier, here + lax.rem(rank + step, quarter))

    @pl.loop(0, quarter)
    def _(step):
        signal(barrier, sibling + lax.rem(rank + step, quarter))

    @pl.when(central)
    def _():
        @pl.loop(0, quarter)
        def _(step):
            signal(barrier, far_center + lax.rem(rank + step, quarter))

    pl.semaphore_wait(barrier, jnp.where(central, 3 * quarter - 1, 2 * quarter - 1))

    def send_level(number, base, first, same):
        group, which, halved = GROUPS[number]

        def sends():
            @pl.loop(first, quarter)
            def _(step):
                peer = base + lax.rem(rank + step, quarter)
                owner = lax.rem(peer, half) if halved else peer
                for at in group:
                    if halved and at == group[0] and not same:
                        continue
                    slot = slot_of(group, which, halved, at, side if same else 1 - side)
                    send(at, owner, slot, peer, send_sem if same else far_sem)

        if which == 3 and not same:
            pl.when(near)(sends)
        else:
            sends()

    order = (0, 1, 2, 3)
    lead = order[0]

    @pl.when(central)
    def _():
        signal(stage_sem.at[0], sibling + rank)
        signal(stage_sem.at[1], far_center + rank)
        send_level(lead, far_center, 0, False)

    send_level(lead, sibling, 0, True)
    send_level(lead, here, 1, True)

    @pl.when(central)
    def _():
        pl.semaphore_wait(stage_sem.at[1], 1)
        signal(stage_sem.at[2], sibling + rank)

    @pl.when(jnp.logical_not(central))
    def _():
        pl.semaphore_wait(stage_sem.at[0], 1)
        send_level(lead, far_center, 0, False)
        pl.semaphore_wait(stage_sem.at[2], 1)

    send_level(lead, far_edge, 0, False)
    send_level(1, far_center, 0, False)
    send_level(1, far_edge, 0, False)
    send_level(2, far_center, 0, False)
    send_level(2, far_edge, 0, False)
    send_level(3, far_center, 0, False)
    send_level(3, far_edge, 0, False)
    send_level(1, sibling, 0, True)
    send_level(1, here, 1, True)
    send_level(2, sibling, 0, True)
    send_level(2, here, 1, True)
    send_level(3, sibling, 0, True)
    send_level(3, here, 1, True)

    video_valid = video_length[0]
    audio_valid = audio_length[0]
    shift = align_offset[0]
    video_rows = arrays[0].shape[0]
    audio_rows = arrays[3].shape[0]
    video_total = n * video_rows
    audio_total = n * audio_rows
    video_reach = video_total // 8
    audio_reach = 5 * audio_total // 8

    def query_places(count, copies, first):
        rows = first + lax.broadcasted_iota(jnp.int32, (count, 1), 0)
        return jnp.concatenate([rows] * copies, axis=0)

    def key_places(count):
        return lax.broadcasted_iota(jnp.int32, (1, count), 1)

    def permit_of(which, copies):
        if which == 0:
            return key_places(video_total) < video_valid
        if which == 1:
            return key_places(audio_total) < audio_valid
        if which == 2:
            where = key_places(audio_total)
            spots = query_places(half * video_rows, copies, side * half * video_rows)
            spots = lax.shift_right_logical(spots, ratio.bit_length() - 1)
            center = jnp.clip(spots + shift, 0, audio_valid - 1)
            return (where < audio_valid) & (jnp.abs(where - center) <= audio_reach)
        where = key_places((half + margin) * video_rows) + side * (half - margin) * video_rows
        spots = query_places(half * audio_rows, copies, side * half * audio_rows)
        center = jnp.clip((spots - shift) * ratio, 0, video_valid - 1)
        return (where < video_valid) & (jnp.abs(where - center) <= video_reach)

    def compute(number):
        group, which, halved = GROUPS[number]
        for at in group:
            pltpu.make_async_copy(held[at], held[at], recv_sem.at[at]).wait()
        query, keys, values = (held[at] for at in group)
        depth = HDV if which == 0 else HDA
        copies = LANES // depth
        scale = 1.0 / math.sqrt(depth)
        permit = permit_of(which, copies)
        for column in range(0, query.shape[2], LANES):
            tokens = read_tokens(query, column)
            if copies > 1:
                lane = lax.broadcasted_iota(jnp.int32, tokens.shape, 1) // depth
                zero = jnp.zeros_like(tokens)
                tokens = jnp.concatenate(
                    [jnp.where(lane == head, tokens, zero) for head in range(copies)], axis=0
                )
            mixed = softmax_mix(
                tokens, read_tokens(keys, column), read_tokens(values, column), permit, scale
            )
            if copies > 1:
                rows = mixed.shape[0] // copies
                merged = mixed[:rows]
                lane = lax.broadcasted_iota(jnp.int32, merged.shape, 1) // depth
                for head in range(1, copies):
                    merged = jnp.where(lane == head, mixed[head * rows : (head + 1) * rows], merged)
                mixed = merged
            write_tokens(results[which], column, mixed)

    def give_back(number):
        group, which, halved = GROUPS[number]
        mine = inner if halved else me
        target = outs[which].at[:, columns(results[which].shape[2], mine)]

        def give(block, peer):
            pltpu.make_async_remote_copy(
                src_ref=results[which].at[block],
                dst_ref=target,
                send_sem=back_send.at[which],
                recv_sem=back_recv.at[which],
                device_id={"seq": peer},
                device_id_type=pl.DeviceIdType.MESH,
            ).start()

        if not halved:

            @pl.loop(0, half)
            def _(step):
                peer = (1 - side) * half + step
                give(peer, peer)

        @pl.loop(1, half)
        def _(step):
            block = lax.rem(inner + step, half)
            peer = side * half + block
            give(block if halved else peer, peer)

        pltpu.make_async_copy(results[which].at[mine], target, back_recv.at[which]).start()

    compute(0)
    compute(1)
    compute(2)
    give_back(2)
    give_back(0)
    give_back(1)
    compute(3)
    give_back(3)

    for which in range(4):
        pltpu.make_async_copy(outs[which], outs[which], back_recv.at[which]).wait()

    def wait_bytes(ref, blocks, sem):
        part = ref.at[pl.ds(0, blocks)]
        pltpu.make_async_copy(part, part, sem).wait()

    for group, which, halved in GROUPS:
        for at in group:
            wait_bytes(held[at], half - 1, send_sem.at[at])
            if not halved or (which == 2 and at != group[0]):
                wait_bytes(held[at], half, far_sem.at[at])
            elif at != group[0]:

                @pl.when(near)
                def _(at=at):
                    wait_bytes(held[at], half, far_sem.at[at])

    for which in range(4):
        wait_bytes(results[which], results[which].shape[0] - 1, back_send.at[which])


def write_out(*refs):
    sources, targets, sem = refs[:4], refs[4:8], refs[8]
    copies = [pltpu.make_async_copy(*pair, sem.at[at]) for at, pair in enumerate(zip(sources, targets))]
    for copy in copies:
        copy.start()
    for copy in copies:
        copy.wait()


def fused_shards(*arguments):
    n = lax.axis_size("seq")
    arrays = arguments[:12]
    lengths = arguments[12:]
    arrays = [pltpu.with_memory_space_constraint(a, pltpu.HBM) for a in arrays]
    ratio = arrays[0].shape[0] // arrays[3].shape[0]
    held = [pltpu.VMEM(s, a.dtype) for s, a in zip(held_shapes(n, arrays), arrays)]
    results = [
        pltpu.VMEM((n, *held[0].shape[1:]), jnp.bfloat16),
        pltpu.VMEM((n, *held[3].shape[1:]), jnp.bfloat16),
        pltpu.VMEM((n // 2, *held[6].shape[1:]), jnp.bfloat16),
        pltpu.VMEM((n // 2, *held[9].shape[1:]), jnp.bfloat16),
    ]
    shapes = [arrays[at].shape for at in (0, 3, 6, 9)]
    anywhere = pl.BlockSpec(memory_space=pl.ANY)
    scalars = pl.BlockSpec(memory_space=pltpu.SMEM)
    vectors = pl.BlockSpec(memory_space=pltpu.VMEM)
    mixed = pl.pallas_call(
        functools.partial(fused_kernel, n, ratio),
        out_shape=tuple(pltpu.VMEM(shape, jnp.bfloat16) for shape in shapes),
        in_specs=[scalars] * 3 + [pl.BlockSpec(memory_space=pltpu.HBM)] * 12,
        out_specs=(vectors,) * 4,
        scratch_shapes=held
        + results
        + [
            pltpu.SemaphoreType.DMA((12,)),
            pltpu.SemaphoreType.DMA((12,)),
            pltpu.SemaphoreType.DMA((12,)),
            pltpu.SemaphoreType.DMA((4,)),
            pltpu.SemaphoreType.DMA((4,)),
            pltpu.SemaphoreType.REGULAR((3,)),
        ],
        compiler_params=pltpu.CompilerParams(
            collective_id=0, has_side_effects=True, vmem_limit_bytes=24 * 2**20
        ),
    )(*lengths, *arrays)
    return pl.pallas_call(
        write_out,
        out_shape=tuple(jax.ShapeDtypeStruct(shape, jnp.bfloat16) for shape in shapes),
        in_specs=[vectors] * 4,
        out_specs=(anywhere,) * 4,
        scratch_shapes=[pltpu.SemaphoreType.DMA((4,))],
        compiler_params=pltpu.CompilerParams(vmem_limit_bytes=2**20),
    )(*mixed)


def kernel_fits(n, video_rows, audio_rows):
    if n < 4 or n % 4 or HV % n or HA % n or (HV // n * HDV) % LANES or (HA // n * HDA) % LANES:
        return False
    ratio = video_rows // audio_rows
    return video_rows == ratio * audio_rows and ratio & (ratio - 1) == 0 and n * audio_rows % 16 == 0 and audio_rows % 8 == 0


def dispatch(*arguments):
    fits = kernel_fits(lax.axis_size("seq"), arguments[0].shape[0], arguments[3].shape[0])
    return (fused_shards if fits else shards)(*arguments)


def solution(mesh):
    placed = (
        P(("clip", "seq"), None),
        P(("clip", "seq"), None),
        P(("clip", "seq"), None),
        P(("clip", "seq"), None),
        P(("clip", "seq"), None),
        P(("clip", "seq"), None),
        P(("clip", "seq"), None),
        P(("clip", "seq"), None),
        P(("clip", "seq"), None),
        P(("clip", "seq"), None),
        P(("clip", "seq"), None),
        P(("clip", "seq"), None),
        P("clip"),
        P("clip"),
        P("clip"),
    )
    return jax.shard_map(
        dispatch,
        mesh=mesh,
        in_specs=placed,
        out_specs=(
            P(("clip", "seq"), None),
            P(("clip", "seq"), None),
            P(("clip", "seq"), None),
            P(("clip", "seq"), None),
        ),
        check_vma=False,
    )
```

```python
import contextlib
import functools
import math

import jax
import jax.numpy as jnp
from jax import lax
from jax.experimental import pallas as pl
from jax.experimental.pallas import tpu as pltpu
from jax.sharding import PartitionSpec as P

HV = 32
HDV = 128
HA = 32
HDA = 64


def block_size(total, limit):
    chosen = min(total, limit)
    while total % chosen:
        chosen -= 1
    return chosen


def split_heads(tokens, heads, depth, copies):
    rows = tokens.shape[0]
    shaped = tokens.reshape(copies, rows // copies, heads, depth).transpose(2, 0, 1, 3)
    return shaped.reshape(heads * copies, rows // copies, depth)


def spread_heads(tokens, heads, depth, copies):
    rows = tokens.shape[0]
    shaped = tokens.reshape(rows, heads, depth).transpose(1, 0, 2)
    shaped = jnp.broadcast_to(shaped[:, None], (heads, copies, rows, depth))
    return shaped.reshape(heads * copies, rows, depth)


def join_heads(owned, heads, depth, copies):
    part_rows = owned.shape[1]
    shaped = owned.reshape(heads, copies, part_rows, depth).transpose(1, 2, 0, 3)
    return shaped.reshape(copies * part_rows, heads * depth)


def owned_positions(rows, copies, devices, index):
    part_rows = rows // copies
    flat = jnp.arange(devices * part_rows, dtype=jnp.int32)
    return flat // part_rows * rows + index % copies * part_rows + flat % part_rows


def online_update(carry, scores, permit, value_tile, value_form):
    running, total, accum = carry
    scores = jnp.where(permit, scores, -1e30)
    newmax = jnp.maximum(running, jnp.max(scores, axis=2))
    weights = jnp.where(permit, jnp.exp(scores - newmax[:, :, None]), 0.0)
    factor = jnp.exp(running - newmax)
    total = total * factor + jnp.sum(weights, axis=2)
    mixed = jnp.einsum(
        value_form, weights.astype(jnp.bfloat16), value_tile, preferred_element_type=jnp.float32
    )
    accum = accum * factor[:, :, None] + mixed
    return (newmax, total, accum)


def fold_initial(rows, heads, depth):
    return (
        jnp.full((heads, rows), -1e30, jnp.float32),
        jnp.zeros((heads, rows), jnp.float32),
        jnp.zeros((heads, rows, depth), jnp.float32),
    )


def fold_piece(carry, local_query, key_rows, value_rows, permit, heads, depth):
    keyed = key_rows.reshape(key_rows.shape[0], heads, depth)
    valued = value_rows.reshape(value_rows.shape[0], heads, depth)
    scores = jnp.einsum("qhd,khd->hqk", local_query, keyed, preferred_element_type=jnp.float32) * (
        1.0 / math.sqrt(depth)
    )
    return online_update(carry, scores, permit[None], valued, "hqk,khd->hqd")


def fold_finish(carry, heads, depth):
    running, total, accum = carry
    result = (accum / total[:, :, None]).astype(jnp.bfloat16)
    return result.transpose(1, 0, 2).reshape(result.shape[1], heads * depth)


def attend_local(queries, keys, values, query_pos, key_pos, allowed):
    heads, q_count, depth = queries.shape
    k_count = keys.shape[1]
    q_block = block_size(q_count, 512)
    k_block = block_size(k_count, 2048)
    scale = 1.0 / math.sqrt(depth)
    q_tiles = queries.reshape(heads, q_count // q_block, q_block, depth).transpose(1, 0, 2, 3)
    k_tiles = keys.reshape(heads, k_count // k_block, k_block, depth).transpose(1, 0, 2, 3)
    v_tiles = values.reshape(heads, k_count // k_block, k_block, depth).transpose(1, 0, 2, 3)
    q_places = query_pos.reshape(q_count // q_block, q_block)
    k_places = key_pos.reshape(k_count // k_block, k_block)

    def one_tile(packed):
        q_tile, q_where = packed

        def absorb(carry, piece):
            k_tile, v_tile, k_where = piece
            scores = (
                jnp.einsum("hqd,hkd->hqk", q_tile, k_tile, preferred_element_type=jnp.float32)
                * scale
            )
            permit = allowed(q_where[:, None], k_where[None, :])[None]
            return (online_update(carry, scores, permit, v_tile, "hqk,hkd->hqd"), None)

        initial = fold_initial(q_block, heads, depth)
        final_state, unused = lax.scan(absorb, initial, (k_tiles, v_tiles, k_places))
        running, total, accum = final_state
        return (accum / total[:, :, None]).astype(jnp.bfloat16)

    tiles = lax.map(one_tile, (q_tiles, q_places))
    return tiles.transpose(1, 0, 2, 3).reshape(heads, q_count, depth)


def shards(
    video_query,
    video_keys,
    video_values,
    audio_query,
    audio_keys,
    audio_values,
    cross_video_query,
    cross_video_keys,
    cross_video_values,
    cross_audio_query,
    cross_audio_keys,
    cross_audio_values,
    video_length,
    audio_length,
    align_offset,
):
    devices = lax.axis_size("seq")
    index = lax.axis_index("seq")
    video_rows = video_query.shape[0]
    audio_rows = audio_query.shape[0]
    video_total = video_rows * devices
    audio_total = audio_rows * devices
    video_reach = video_total // 8
    audio_reach = 5 * audio_total // 8
    video_valid = video_length[0]
    audio_valid = audio_length[0]
    align_shift = align_offset[0]
    copies = max(devices // HV, 1)
    video_places = jnp.arange(video_total, dtype=jnp.int32)
    audio_places = jnp.arange(audio_total, dtype=jnp.int32)

    def video_open(q_where, k_where):
        return k_where < video_valid

    def toward_video(q_where, k_where):
        center = jnp.clip(q_where * audio_total // video_total + align_shift, 0, audio_valid - 1)
        return (k_where < audio_valid) & (jnp.abs(k_where - center) <= audio_reach)

    def toward_audio(q_where, k_where):
        center = jnp.clip((q_where - align_shift) * video_total // audio_total, 0, video_valid - 1)
        return (k_where < video_valid) & (jnp.abs(k_where - center) <= video_reach)

    video_owned = (
        lax.all_to_all(
            split_heads(video_query, HV, HDV, copies),
            "seq",
            split_axis=0,
            concat_axis=1,
            tiled=True,
        ),
        lax.all_to_all(
            spread_heads(video_keys, HV, HDV, copies),
            "seq",
            split_axis=0,
            concat_axis=1,
            tiled=True,
        ),
        lax.all_to_all(
            spread_heads(video_values, HV, HDV, copies),
            "seq",
            split_axis=0,
            concat_axis=1,
            tiled=True,
        ),
    )
    video_done = attend_local(
        video_owned[0],
        video_owned[1],
        video_owned[2],
        owned_positions(video_rows, copies, devices, index),
        video_places,
        video_open,
    )
    video_mixed = join_heads(
        lax.all_to_all(video_done, "seq", split_axis=1, concat_axis=0, tiled=True), HV, HDV, copies
    )
    audio_local = audio_query.reshape(audio_rows, HA, HDA)
    piece = (
        lax.all_gather(audio_keys, "seq", axis=0, tiled=True),
        lax.all_gather(audio_values, "seq", axis=0, tiled=True),
    )
    k_where = jnp.arange(piece[0].shape[0], dtype=jnp.int32)
    audio_k_where = k_where[None, :]
    permit = audio_k_where < audio_valid
    audio_state = fold_piece(
        fold_initial(audio_rows, HA, HDA), audio_local, piece[0], piece[1], permit, HA, HDA
    )
    audio_mixed = fold_finish(audio_state, HA, HDA)
    cross_owned = (
        lax.all_to_all(
            split_heads(cross_video_query, HA, HDA, copies),
            "seq",
            split_axis=0,
            concat_axis=1,
            tiled=True,
        ),
        lax.all_to_all(
            spread_heads(cross_audio_keys, HA, HDA, copies),
            "seq",
            split_axis=0,
            concat_axis=1,
            tiled=True,
        ),
        lax.all_to_all(
            spread_heads(cross_audio_values, HA, HDA, copies),
            "seq",
            split_axis=0,
            concat_axis=1,
            tiled=True,
        ),
    )
    cross_done = attend_local(
        cross_owned[0],
        cross_owned[1],
        cross_owned[2],
        owned_positions(video_rows, copies, devices, index),
        audio_places,
        toward_video,
    )
    video_cross = join_heads(
        lax.all_to_all(cross_done, "seq", split_axis=1, concat_axis=0, tiled=True), HA, HDA, copies
    )
    listen_owned = (
        lax.all_to_all(
            split_heads(cross_audio_query, HA, HDA, copies),
            "seq",
            split_axis=0,
            concat_axis=1,
            tiled=True,
        ),
        lax.all_to_all(
            spread_heads(cross_video_keys, HA, HDA, copies),
            "seq",
            split_axis=0,
            concat_axis=1,
            tiled=True,
        ),
        lax.all_to_all(
            spread_heads(cross_video_values, HA, HDA, copies),
            "seq",
            split_axis=0,
            concat_axis=1,
            tiled=True,
        ),
    )
    listen_done = attend_local(
        listen_owned[0],
        listen_owned[1],
        listen_owned[2],
        owned_positions(audio_rows, copies, devices, index),
        video_places,
        toward_audio,
    )
    audio_cross = join_heads(
        lax.all_to_all(listen_done, "seq", split_axis=1, concat_axis=0, tiled=True), HA, HDA, copies
    )
    return (video_mixed, audio_mixed, video_cross, audio_cross)


LANES = 128
mark = lambda name: contextlib.nullcontext()

GROUPS = (
    ((0, 1, 2), 0, False),
    ((3, 4, 5), 1, False),
    ((6, 10, 11), 2, True),
    ((9, 7, 8), 3, True),
)


def softmax_mix(query, keys, values, permit, scale):
    scores = lax.dot_general(
        query, keys, (((1,), (1,)), ((), ())), preferred_element_type=jnp.float32
    )
    scores = jnp.where(permit, scores * scale, -1e30)
    peak = jnp.max(scores, axis=1, keepdims=True)
    weights = jnp.exp(scores - peak)
    total = jnp.sum(weights, axis=1, keepdims=True)
    mixed = jnp.dot(weights.astype(jnp.bfloat16), values, preferred_element_type=jnp.float32)
    return mixed / total


def read_tokens(ref, column):
    block = ref[:, :, column : column + LANES]
    n, rows, _ = block.shape
    if rows % 16:
        return block.astype(jnp.float32).reshape(n * rows, LANES).astype(block.dtype)
    return block.reshape(n * rows, LANES)


def write_tokens(ref, column, result):
    n, rows, _ = ref.shape
    ref[:, :, column : column + LANES] = result.reshape(n, rows, LANES).astype(ref.dtype)


def margin_blocks(n, video_rows):
    return min(-(-(3 * n * video_rows // 16) // video_rows), n // 2)


def held_shapes(n, arrays):
    half = n // 2
    shapes = [None] * 12
    for group, which, halved in GROUPS:
        for place, at in enumerate(group):
            rows, cols = arrays[at].shape
            blocks = n
            if halved and place == 0:
                blocks = half
            elif which == 3:
                blocks = half + margin_blocks(n, rows)
            shapes[at] = (blocks, rows, cols // (half if halved else n))
    return shapes


def fused_kernel(n, ratio, *refs):
    video_length, audio_length, align_offset = refs[:3]
    arrays = refs[3:15]
    outs = refs[15:19]
    held = refs[19:31]
    results = refs[31:35]
    send_sem, far_sem, recv_sem, back_send, back_recv, stage_sem = refs[35:]
    half = n // 2
    quarter = n // 4
    margin = held[7].shape[0] - half
    me = lax.axis_index("seq")
    side = me // half
    inner = lax.rem(me, half)
    near = (me >= half - margin) & (me < half + margin)

    def columns(width, owner):
        return pl.ds(pl.multiple_of(owner * width, LANES), width)

    def slot_of(group, which, halved, at, to_side):
        if halved and at == group[0]:
            return inner
        if which == 3:
            return me - to_side * (half - margin)
        return me

    def send(at, owner, slot, peer, sem):
        pltpu.make_async_remote_copy(
            src_ref=arrays[at].at[:, columns(held[at].shape[2], owner)],
            dst_ref=held[at].at[slot],
            send_sem=sem.at[at],
            recv_sem=recv_sem.at[at],
            device_id={"seq": peer},
            device_id_type=pl.DeviceIdType.MESH,
        ).start()

    for group, which, halved in GROUPS:
        for at in group:
            pltpu.make_async_copy(
                arrays[at].at[:, columns(held[at].shape[2], inner if halved else me)],
                held[at].at[slot_of(group, which, halved, at, side)],
                recv_sem.at[at],
            ).start()

    col = quarter // 2
    level = me // quarter
    rank = lax.rem(me, quarter)
    core = lax.rem(rank, col)
    mine_col = rank - core
    next_col = col - mine_col
    central = (level == 1) | (level == 2)
    here = level * quarter
    sibling = (level + 1 - 2 * lax.rem(level, 2)) * quarter
    far_center = (2 - side) * quarter
    far_edge = (3 - 3 * side) * quarter

    barrier = pltpu.get_barrier_semaphore()

    def signal(sem, peer):
        pl.semaphore_signal(
            sem, inc=1, device_id={"seq": peer}, device_id_type=pl.DeviceIdType.MESH
        )

    def greet(base, first):
        @pl.loop(first, col)
        def _(step):
            signal(barrier, base + lax.rem(core + step, col))

    @pl.when(central)
    def _():
        greet(far_center + mine_col, 0)

    greet(here + mine_col, 1)

    @pl.when(central)
    def _():
        greet(here + next_col, 0)
        greet(sibling + mine_col, 0)

    with mark("BAR"):
        pl.semaphore_wait(barrier, jnp.where(central, 3 * col - 1, 2 * col - 1))

    def send_part(number, base, count, first, same):
        group, which, halved = GROUPS[number]
        spot = core if count == col else rank

        def sends():
            @pl.loop(first, count)
            def _(step):
                peer = base + lax.rem(spot + step, count)
                owner = lax.rem(peer, half) if halved else peer
                for at in group:
                    if halved and at == group[0] and not same:
                        continue
                    slot = slot_of(group, which, halved, at, side if same else 1 - side)
                    send(at, owner, slot, peer, send_sem if same else far_sem)

        if which == 3 and not same:
            pl.when(near)(sends)
        else:
            sends()

    def f(number):
        send_part(number, far_edge, quarter, 0, False)
        send_part(number, far_center, quarter, 0, False)

    def s(number):
        send_part(number, sibling, quarter, 0, True)

    def h(number):
        send_part(number, here, quarter, 1, True)

    across = rank + next_col - mine_col

    @pl.when(central)
    def _():
        signal(stage_sem.at[0], here + across)
        send_part(0, far_center + mine_col, col, 0, False)
        h(0)
        with mark("Y"):
            pl.semaphore_wait(stage_sem.at[0], 1)
        send_part(0, far_center + next_col, col, 0, False)
        with mark("O"):
            pl.semaphore_wait(stage_sem.at[2], 1)
        signal(stage_sem.at[1], sibling + rank)
        signal(stage_sem.at[5], here + across)
        with mark("Y2"):
            pl.semaphore_wait(stage_sem.at[5], 1)
        signal(stage_sem.at[3], far_center + rank)
        s(0)
        with mark("B"):
            pl.semaphore_wait(stage_sem.at[3], 1)
        signal(stage_sem.at[4], sibling + rank)
        send_part(0, far_edge, quarter, 0, False)
        f(1)
        f(3)
        f(2)
        h(1)
        s(1)
        h(3)
        s(3)
        h(2)
        s(2)

    @pl.when(jnp.logical_not(central))
    def _():
        signal(stage_sem.at[2], sibling + rank)
        send_part(0, sibling + mine_col, col, 0, True)
        send_part(0, here + mine_col, col, 1, True)
        with mark("A"):
            pl.semaphore_wait(stage_sem.at[1], 1)
        send_part(0, sibling + next_col, col, 0, True)
        send_part(0, far_center, quarter, 0, False)
        with mark("C"):
            pl.semaphore_wait(stage_sem.at[4], 1)
        send_part(0, far_edge, quarter, 0, False)
        send_part(0, here + next_col, col, 0, True)
        f(1)
        s(1)
        s(3)
        f(2)
        s(2)
        h(1)
        h(3)
        h(2)

    video_valid = video_length[0]
    audio_valid = audio_length[0]
    shift = align_offset[0]
    video_rows = arrays[0].shape[0]
    audio_rows = arrays[3].shape[0]
    video_total = n * video_rows
    audio_total = n * audio_rows
    video_reach = video_total // 8
    audio_reach = 5 * audio_total // 8

    def query_places(count, copies, first):
        rows = first + lax.broadcasted_iota(jnp.int32, (count, 1), 0)
        return jnp.concatenate([rows] * copies, axis=0)

    def key_places(count):
        return lax.broadcasted_iota(jnp.int32, (1, count), 1)

    def permit_of(which, copies):
        if which == 0:
            return key_places(video_total) < video_valid
        if which == 1:
            return key_places(audio_total) < audio_valid
        if which == 2:
            where = key_places(audio_total)
            spots = query_places(half * video_rows, copies, side * half * video_rows)
            spots = lax.shift_right_logical(spots, ratio.bit_length() - 1)
            center = jnp.clip(spots + shift, 0, audio_valid - 1)
            return (where < audio_valid) & (jnp.abs(where - center) <= audio_reach)
        where = key_places((half + margin) * video_rows) + side * (half - margin) * video_rows
        spots = query_places(half * audio_rows, copies, side * half * audio_rows)
        center = jnp.clip((spots - shift) * ratio, 0, video_valid - 1)
        return (where < video_valid) & (jnp.abs(where - center) <= video_reach)

    def compute(number):
        group, which, halved = GROUPS[number]
        for at in group:
            with mark("W%d_%d" % (which, at)):
                pltpu.make_async_copy(held[at], held[at], recv_sem.at[at]).wait()
        query, keys, values = (held[at] for at in group)
        depth = HDV if which == 0 else HDA
        copies = LANES // depth
        scale = 1.0 / math.sqrt(depth)
        permit = permit_of(which, copies)
        for column in range(0, query.shape[2], LANES):
            tokens = read_tokens(query, column)
            if copies > 1:
                lane = lax.broadcasted_iota(jnp.int32, tokens.shape, 1) // depth
                zero = jnp.zeros_like(tokens)
                tokens = jnp.concatenate(
                    [jnp.where(lane == head, tokens, zero) for head in range(copies)], axis=0
                )
            mixed = softmax_mix(
                tokens, read_tokens(keys, column), read_tokens(values, column), permit, scale
            )
            if copies > 1:
                rows = mixed.shape[0] // copies
                merged = mixed[:rows]
                lane = lax.broadcasted_iota(jnp.int32, merged.shape, 1) // depth
                for head in range(1, copies):
                    merged = jnp.where(lane == head, mixed[head * rows : (head + 1) * rows], merged)
                mixed = merged
            write_tokens(results[which], column, mixed)

    def give_back(number, far=False, close=False):
        group, which, halved = GROUPS[number]
        mine = inner if halved else me
        target = outs[which].at[:, columns(results[which].shape[2], mine)]

        def give(block, peer):
            pltpu.make_async_remote_copy(
                src_ref=results[which].at[block],
                dst_ref=target,
                send_sem=back_send.at[which],
                recv_sem=back_recv.at[which],
                device_id={"seq": peer},
                device_id_type=pl.DeviceIdType.MESH,
            ).start()

        if far:

            @pl.loop(0, half)
            def _(step):
                peer = (1 - side) * half + step
                give(peer, peer)

        if not close:
            return

        @pl.loop(1, half)
        def _(step):
            block = lax.rem(inner + step, half)
            peer = side * half + block
            give(block if halved else peer, peer)

        pltpu.make_async_copy(results[which].at[mine], target, back_recv.at[which]).start()

    compute(0)
    give_back(0, close=True)
    pl.when(central)(lambda: give_back(0, far=True))
    compute(1)
    give_back(1, close=True)
    pl.when(central)(lambda: give_back(1, far=True))
    compute(3)
    give_back(3, far=False, close=True)
    pl.when(jnp.logical_not(central))(lambda: give_back(0, far=True))
    pl.when(jnp.logical_not(central))(lambda: give_back(1, far=True))
    compute(2)
    give_back(2, far=False, close=True)

    for which in range(4):
        with mark("R%d" % which):
            pltpu.make_async_copy(outs[which], outs[which], back_recv.at[which]).wait()

    def wait_bytes(ref, blocks, sem):
        part = ref.at[pl.ds(0, blocks)]
        pltpu.make_async_copy(part, part, sem).wait()

    for group, which, halved in GROUPS:
        for at in group:
            wait_bytes(held[at], half - 1, send_sem.at[at])
            if not halved or (which == 2 and at != group[0]):
                wait_bytes(held[at], half, far_sem.at[at])
            elif at != group[0]:

                @pl.when(near)
                def _(at=at):
                    wait_bytes(held[at], half, far_sem.at[at])

    for which in range(4):
        wait_bytes(results[which], results[which].shape[0] - 1, back_send.at[which])


def write_out(*refs):
    sources, targets, sem = refs[:4], refs[4:8], refs[8]
    copies = [pltpu.make_async_copy(*pair, sem.at[at]) for at, pair in enumerate(zip(sources, targets))]
    for copy in copies:
        copy.start()
    for copy in copies:
        copy.wait()


def fused_shards(*arguments):
    n = lax.axis_size("seq")
    arrays = arguments[:12]
    lengths = arguments[12:]
    arrays = [pltpu.with_memory_space_constraint(a, pltpu.HBM) for a in arrays]
    ratio = arrays[0].shape[0] // arrays[3].shape[0]
    held = [pltpu.VMEM(s, a.dtype) for s, a in zip(held_shapes(n, arrays), arrays)]
    results = [
        pltpu.VMEM((n, *held[0].shape[1:]), jnp.bfloat16),
        pltpu.VMEM((n, *held[3].shape[1:]), jnp.bfloat16),
        pltpu.VMEM((n // 2, *held[6].shape[1:]), jnp.bfloat16),
        pltpu.VMEM((n // 2, *held[9].shape[1:]), jnp.bfloat16),
    ]
    shapes = [arrays[at].shape for at in (0, 3, 6, 9)]
    anywhere = pl.BlockSpec(memory_space=pl.ANY)
    scalars = pl.BlockSpec(memory_space=pltpu.SMEM)
    vectors = pl.BlockSpec(memory_space=pltpu.VMEM)
    mixed = pl.pallas_call(
        functools.partial(fused_kernel, n, ratio),
        out_shape=tuple(pltpu.VMEM(shape, jnp.bfloat16) for shape in shapes),
        in_specs=[scalars] * 3 + [pl.BlockSpec(memory_space=pltpu.HBM)] * 12,
        out_specs=(vectors,) * 4,
        scratch_shapes=held
        + results
        + [
            pltpu.SemaphoreType.DMA((12,)),
            pltpu.SemaphoreType.DMA((12,)),
            pltpu.SemaphoreType.DMA((12,)),
            pltpu.SemaphoreType.DMA((4,)),
            pltpu.SemaphoreType.DMA((4,)),
            pltpu.SemaphoreType.REGULAR((6,)),
        ],
        compiler_params=pltpu.CompilerParams(
            collective_id=0, has_side_effects=True, vmem_limit_bytes=24 * 2**20
        ),
    )(*lengths, *arrays)
    return pl.pallas_call(
        write_out,
        out_shape=tuple(jax.ShapeDtypeStruct(shape, jnp.bfloat16) for shape in shapes),
        in_specs=[vectors] * 4,
        out_specs=(anywhere,) * 4,
        scratch_shapes=[pltpu.SemaphoreType.DMA((4,))],
        compiler_params=pltpu.CompilerParams(vmem_limit_bytes=2**20),
    )(*mixed)


def kernel_fits(n, video_rows, audio_rows):
    if n % 16 or HV % n or HA % n or (HV // n * HDV) % LANES or (HA // n * HDA) % LANES:
        return False
    ratio = video_rows // audio_rows
    return video_rows == ratio * audio_rows and ratio & (ratio - 1) == 0 and n * audio_rows % 16 == 0 and audio_rows % 8 == 0


def dispatch(*arguments):
    fits = kernel_fits(lax.axis_size("seq"), arguments[0].shape[0], arguments[3].shape[0])
    return (fused_shards if fits else shards)(*arguments)


def solution(mesh):
    placed = (
        P(("clip", "seq"), None),
        P(("clip", "seq"), None),
        P(("clip", "seq"), None),
        P(("clip", "seq"), None),
        P(("clip", "seq"), None),
        P(("clip", "seq"), None),
        P(("clip", "seq"), None),
        P(("clip", "seq"), None),
        P(("clip", "seq"), None),
        P(("clip", "seq"), None),
        P(("clip", "seq"), None),
        P(("clip", "seq"), None),
        P("clip"),
        P("clip"),
        P("clip"),
    )
    return jax.shard_map(
        dispatch,
        mesh=mesh,
        in_specs=placed,
        out_specs=(
            P(("clip", "seq"), None),
            P(("clip", "seq"), None),
            P(("clip", "seq"), None),
            P(("clip", "seq"), None),
        ),
        check_vma=False,
    )
```

```python
import contextlib
import functools
import math

import jax
import jax.numpy as jnp
from jax import lax
from jax.experimental import pallas as pl
from jax.experimental.pallas import tpu as pltpu
from jax.sharding import PartitionSpec as P

HV = 32
HDV = 128
HA = 32
HDA = 64


def block_size(total, limit):
    chosen = min(total, limit)
    while total % chosen:
        chosen -= 1
    return chosen


def split_heads(tokens, heads, depth, copies):
    rows = tokens.shape[0]
    shaped = tokens.reshape(copies, rows // copies, heads, depth).transpose(2, 0, 1, 3)
    return shaped.reshape(heads * copies, rows // copies, depth)


def spread_heads(tokens, heads, depth, copies):
    rows = tokens.shape[0]
    shaped = tokens.reshape(rows, heads, depth).transpose(1, 0, 2)
    shaped = jnp.broadcast_to(shaped[:, None], (heads, copies, rows, depth))
    return shaped.reshape(heads * copies, rows, depth)


def join_heads(owned, heads, depth, copies):
    part_rows = owned.shape[1]
    shaped = owned.reshape(heads, copies, part_rows, depth).transpose(1, 2, 0, 3)
    return shaped.reshape(copies * part_rows, heads * depth)


def owned_positions(rows, copies, devices, index):
    part_rows = rows // copies
    flat = jnp.arange(devices * part_rows, dtype=jnp.int32)
    return flat // part_rows * rows + index % copies * part_rows + flat % part_rows


def online_update(carry, scores, permit, value_tile, value_form):
    running, total, accum = carry
    scores = jnp.where(permit, scores, -1e30)
    newmax = jnp.maximum(running, jnp.max(scores, axis=2))
    weights = jnp.where(permit, jnp.exp(scores - newmax[:, :, None]), 0.0)
    factor = jnp.exp(running - newmax)
    total = total * factor + jnp.sum(weights, axis=2)
    mixed = jnp.einsum(
        value_form, weights.astype(jnp.bfloat16), value_tile, preferred_element_type=jnp.float32
    )
    accum = accum * factor[:, :, None] + mixed
    return (newmax, total, accum)


def fold_initial(rows, heads, depth):
    return (
        jnp.full((heads, rows), -1e30, jnp.float32),
        jnp.zeros((heads, rows), jnp.float32),
        jnp.zeros((heads, rows, depth), jnp.float32),
    )


def fold_piece(carry, local_query, key_rows, value_rows, permit, heads, depth):
    keyed = key_rows.reshape(key_rows.shape[0], heads, depth)
    valued = value_rows.reshape(value_rows.shape[0], heads, depth)
    scores = jnp.einsum("qhd,khd->hqk", local_query, keyed, preferred_element_type=jnp.float32) * (
        1.0 / math.sqrt(depth)
    )
    return online_update(carry, scores, permit[None], valued, "hqk,khd->hqd")


def fold_finish(carry, heads, depth):
    running, total, accum = carry
    result = (accum / total[:, :, None]).astype(jnp.bfloat16)
    return result.transpose(1, 0, 2).reshape(result.shape[1], heads * depth)


def attend_local(queries, keys, values, query_pos, key_pos, allowed):
    heads, q_count, depth = queries.shape
    k_count = keys.shape[1]
    q_block = block_size(q_count, 512)
    k_block = block_size(k_count, 2048)
    scale = 1.0 / math.sqrt(depth)
    q_tiles = queries.reshape(heads, q_count // q_block, q_block, depth).transpose(1, 0, 2, 3)
    k_tiles = keys.reshape(heads, k_count // k_block, k_block, depth).transpose(1, 0, 2, 3)
    v_tiles = values.reshape(heads, k_count // k_block, k_block, depth).transpose(1, 0, 2, 3)
    q_places = query_pos.reshape(q_count // q_block, q_block)
    k_places = key_pos.reshape(k_count // k_block, k_block)

    def one_tile(packed):
        q_tile, q_where = packed

        def absorb(carry, piece):
            k_tile, v_tile, k_where = piece
            scores = (
                jnp.einsum("hqd,hkd->hqk", q_tile, k_tile, preferred_element_type=jnp.float32)
                * scale
            )
            permit = allowed(q_where[:, None], k_where[None, :])[None]
            return (online_update(carry, scores, permit, v_tile, "hqk,hkd->hqd"), None)

        initial = fold_initial(q_block, heads, depth)
        final_state, unused = lax.scan(absorb, initial, (k_tiles, v_tiles, k_places))
        running, total, accum = final_state
        return (accum / total[:, :, None]).astype(jnp.bfloat16)

    tiles = lax.map(one_tile, (q_tiles, q_places))
    return tiles.transpose(1, 0, 2, 3).reshape(heads, q_count, depth)


def shards(
    video_query,
    video_keys,
    video_values,
    audio_query,
    audio_keys,
    audio_values,
    cross_video_query,
    cross_video_keys,
    cross_video_values,
    cross_audio_query,
    cross_audio_keys,
    cross_audio_values,
    video_length,
    audio_length,
    align_offset,
):
    devices = lax.axis_size("seq")
    index = lax.axis_index("seq")
    video_rows = video_query.shape[0]
    audio_rows = audio_query.shape[0]
    video_total = video_rows * devices
    audio_total = audio_rows * devices
    video_reach = video_total // 8
    audio_reach = 5 * audio_total // 8
    video_valid = video_length[0]
    audio_valid = audio_length[0]
    align_shift = align_offset[0]
    copies = max(devices // HV, 1)
    video_places = jnp.arange(video_total, dtype=jnp.int32)
    audio_places = jnp.arange(audio_total, dtype=jnp.int32)

    def video_open(q_where, k_where):
        return k_where < video_valid

    def toward_video(q_where, k_where):
        center = jnp.clip(q_where * audio_total // video_total + align_shift, 0, audio_valid - 1)
        return (k_where < audio_valid) & (jnp.abs(k_where - center) <= audio_reach)

    def toward_audio(q_where, k_where):
        center = jnp.clip((q_where - align_shift) * video_total // audio_total, 0, video_valid - 1)
        return (k_where < video_valid) & (jnp.abs(k_where - center) <= video_reach)

    video_owned = (
        lax.all_to_all(
            split_heads(video_query, HV, HDV, copies),
            "seq",
            split_axis=0,
            concat_axis=1,
            tiled=True,
        ),
        lax.all_to_all(
            spread_heads(video_keys, HV, HDV, copies),
            "seq",
            split_axis=0,
            concat_axis=1,
            tiled=True,
        ),
        lax.all_to_all(
            spread_heads(video_values, HV, HDV, copies),
            "seq",
            split_axis=0,
            concat_axis=1,
            tiled=True,
        ),
    )
    video_done = attend_local(
        video_owned[0],
        video_owned[1],
        video_owned[2],
        owned_positions(video_rows, copies, devices, index),
        video_places,
        video_open,
    )
    video_mixed = join_heads(
        lax.all_to_all(video_done, "seq", split_axis=1, concat_axis=0, tiled=True), HV, HDV, copies
    )
    audio_local = audio_query.reshape(audio_rows, HA, HDA)
    piece = (
        lax.all_gather(audio_keys, "seq", axis=0, tiled=True),
        lax.all_gather(audio_values, "seq", axis=0, tiled=True),
    )
    k_where = jnp.arange(piece[0].shape[0], dtype=jnp.int32)
    audio_k_where = k_where[None, :]
    permit = audio_k_where < audio_valid
    audio_state = fold_piece(
        fold_initial(audio_rows, HA, HDA), audio_local, piece[0], piece[1], permit, HA, HDA
    )
    audio_mixed = fold_finish(audio_state, HA, HDA)
    cross_owned = (
        lax.all_to_all(
            split_heads(cross_video_query, HA, HDA, copies),
            "seq",
            split_axis=0,
            concat_axis=1,
            tiled=True,
        ),
        lax.all_to_all(
            spread_heads(cross_audio_keys, HA, HDA, copies),
            "seq",
            split_axis=0,
            concat_axis=1,
            tiled=True,
        ),
        lax.all_to_all(
            spread_heads(cross_audio_values, HA, HDA, copies),
            "seq",
            split_axis=0,
            concat_axis=1,
            tiled=True,
        ),
    )
    cross_done = attend_local(
        cross_owned[0],
        cross_owned[1],
        cross_owned[2],
        owned_positions(video_rows, copies, devices, index),
        audio_places,
        toward_video,
    )
    video_cross = join_heads(
        lax.all_to_all(cross_done, "seq", split_axis=1, concat_axis=0, tiled=True), HA, HDA, copies
    )
    listen_owned = (
        lax.all_to_all(
            split_heads(cross_audio_query, HA, HDA, copies),
            "seq",
            split_axis=0,
            concat_axis=1,
            tiled=True,
        ),
        lax.all_to_all(
            spread_heads(cross_video_keys, HA, HDA, copies),
            "seq",
            split_axis=0,
            concat_axis=1,
            tiled=True,
        ),
        lax.all_to_all(
            spread_heads(cross_video_values, HA, HDA, copies),
            "seq",
            split_axis=0,
            concat_axis=1,
            tiled=True,
        ),
    )
    listen_done = attend_local(
        listen_owned[0],
        listen_owned[1],
        listen_owned[2],
        owned_positions(audio_rows, copies, devices, index),
        video_places,
        toward_audio,
    )
    audio_cross = join_heads(
        lax.all_to_all(listen_done, "seq", split_axis=1, concat_axis=0, tiled=True), HA, HDA, copies
    )
    return (video_mixed, audio_mixed, video_cross, audio_cross)


LANES = 128
mark = lambda name: contextlib.nullcontext()
KEYED = (7, 8)
PARTIAL = 3

GROUPS = (
    ((0, 1, 2), 0, False),
    ((3, 4, 5), 1, False),
    ((6, 10, 11), 2, True),
    ((9, 7, 8), 3, True),
)


def softmax_mix(query, keys, values, permit, scale):
    scores = lax.dot_general(
        query, keys, (((1,), (1,)), ((), ())), preferred_element_type=jnp.float32
    )
    scores = jnp.where(permit, scores * scale, -1e30)
    peak = jnp.max(scores, axis=1, keepdims=True)
    weights = jnp.exp(scores - peak)
    total = jnp.sum(weights, axis=1, keepdims=True)
    mixed = jnp.dot(weights.astype(jnp.bfloat16), values, preferred_element_type=jnp.float32)
    return mixed / total


def read_tokens(ref, column):
    block = ref[:, :, column : column + LANES]
    n, rows, _ = block.shape
    if rows % 16:
        return block.astype(jnp.float32).reshape(n * rows, LANES).astype(block.dtype)
    return block.reshape(n * rows, LANES)


def write_tokens(ref, column, result):
    n, rows, _ = ref.shape
    ref[:, :, column : column + LANES] = result.reshape(n, rows, LANES).astype(ref.dtype)


def margin_blocks(n, video_rows):
    return min(-(-(3 * n * video_rows // 16) // video_rows), n // 2)


def held_shapes(n, arrays):
    half = n // 2
    shapes = [None] * 12
    for group, which, halved in GROUPS:
        for place, at in enumerate(group):
            rows, cols = arrays[at].shape
            blocks = n
            if halved and place == 0:
                blocks = half
            elif which == 3:
                blocks = half + margin_blocks(n, rows)
            shapes[at] = (blocks, rows, cols // (half if halved else n))
    return shapes


def fused_kernel(n, ratio, *refs):
    video_length, audio_length, align_offset = refs[:3]
    arrays = refs[3:15]
    outs = refs[15:19]
    held = refs[19:31]
    results = refs[31:35]
    send_sem, far_sem, recv_sem, back_send, back_recv, stage_sem, part_sem, guest, part_out, part_in = refs[
        35:
    ]
    half = n // 2
    quarter = n // 4
    margin = held[7].shape[0] - half
    me = lax.axis_index("seq")
    side = me // half
    inner = lax.rem(me, half)
    near = (me >= half - margin) & (me < half + margin)
    lower = side == 0
    upper = side == 1
    hosted = near & lower
    edge_key = near & upper

    def arrival(at, same):
        if at in KEYED and same:
            return recv_sem.at[jnp.where(edge_key, 12 + KEYED.index(at), at)]
        return recv_sem.at[at]

    def columns(width, owner):
        return pl.ds(pl.multiple_of(owner * width, LANES), width)

    def slot_of(group, which, halved, at, to_side):
        if halved and at == group[0]:
            return inner
        if which == 3:
            return me - to_side * (half - margin)
        return me

    def send(at, owner, slot, peer, sem, same):
        pltpu.make_async_remote_copy(
            src_ref=arrays[at].at[:, columns(held[at].shape[2], owner)],
            dst_ref=held[at].at[slot],
            send_sem=sem.at[at],
            recv_sem=arrival(at, same),
            device_id={"seq": peer},
            device_id_type=pl.DeviceIdType.MESH,
        ).start()

    for group, which, halved in GROUPS:
        for at in group:
            pltpu.make_async_copy(
                arrays[at].at[:, columns(held[at].shape[2], inner if halved else me)],
                held[at].at[slot_of(group, which, halved, at, side)],
                arrival(at, True),
            ).start()

    col = quarter // 2
    level = me // quarter
    rank = lax.rem(me, quarter)
    core = lax.rem(rank, col)
    mine_col = rank - core
    next_col = col - mine_col
    central = (level == 1) | (level == 2)
    here = level * quarter
    sibling = (level + 1 - 2 * lax.rem(level, 2)) * quarter
    far_center = (2 - side) * quarter
    far_edge = (3 - 3 * side) * quarter

    barrier = pltpu.get_barrier_semaphore()

    def signal(sem, peer):
        pl.semaphore_signal(
            sem, inc=1, device_id={"seq": peer}, device_id_type=pl.DeviceIdType.MESH
        )

    def greet(base, first):
        @pl.loop(first, col)
        def _(step):
            signal(barrier, base + lax.rem(core + step, col))

    @pl.when(central)
    def _():
        greet(far_center + mine_col, 0)

    greet(here + mine_col, 1)

    @pl.when(central)
    def _():
        greet(here + next_col, 0)
        greet(sibling + mine_col, 0)

    with mark("BAR"):
        pl.semaphore_wait(barrier, jnp.where(central, 3 * col - 1, 2 * col - 1))

    def send_part(number, base, count, first, same):
        group, which, halved = GROUPS[number]
        spot = core if count == col else rank

        def sends():
            @pl.loop(first, count)
            def _(step):
                peer = base + lax.rem(spot + step, count)
                owner = lax.rem(peer, half) if halved else peer
                for at in group:
                    if halved and at == group[0] and not same:
                        continue
                    slot = slot_of(group, which, halved, at, side if same else 1 - side)
                    send(at, owner, slot, peer, send_sem if same else far_sem, same)

        if which == 3 and not same:
            pl.when(hosted)(sends)
        else:
            sends()

    def f(number):
        send_part(number, far_edge, quarter, 0, False)
        send_part(number, far_center, quarter, 0, False)

    def k(number):
        send_part(number, far_center, quarter, 0, False)

    def g(number):
        send_part(number, far_edge, quarter, 0, False)

    def s(number):
        send_part(number, sibling, quarter, 0, True)

    def v(number):
        group = GROUPS[number][0]

        @pl.when(hosted)
        def _():
            @pl.loop(0, half)
            def _(step):
                owner = lax.rem(inner + step, half)
                pltpu.make_async_remote_copy(
                    src_ref=arrays[group[0]].at[:, columns(held[group[0]].shape[2], owner)],
                    dst_ref=guest.at[me - (half - margin)],
                    send_sem=far_sem.at[group[0]],
                    recv_sem=recv_sem.at[14],
                    device_id={"seq": half + owner},
                    device_id_type=pl.DeviceIdType.MESH,
                ).start()

    def h(number):
        send_part(number, here, quarter, 1, True)

    across = rank + next_col - mine_col

    @pl.when(central)
    def _():
        signal(stage_sem.at[0], here + across)
        send_part(0, far_center + mine_col, col, 0, False)
        h(0)
        with mark("Y"):
            pl.semaphore_wait(stage_sem.at[0], 1)
        send_part(0, far_center + next_col, col, 0, False)
        with mark("O"):
            pl.semaphore_wait(stage_sem.at[2], 1)
        signal(stage_sem.at[1], sibling + rank)
        signal(stage_sem.at[5], here + across)
        with mark("Y2"):
            pl.semaphore_wait(stage_sem.at[5], 1)
        signal(stage_sem.at[3], far_center + rank)
        s(0)
        with mark("B"):
            pl.semaphore_wait(stage_sem.at[3], 1)
        signal(stage_sem.at[4], sibling + rank)
        send_part(0, far_edge, quarter, 0, False)
        v(3)
        f(1)
        f(3)
        f(2)
        h(3)
        s(3)
        h(1)
        s(1)
        h(2)
        s(2)

    @pl.when(jnp.logical_not(central))
    def _():
        signal(stage_sem.at[2], sibling + rank)
        send_part(0, sibling + mine_col, col, 0, True)
        send_part(0, here + mine_col, col, 1, True)
        with mark("A"):
            pl.semaphore_wait(stage_sem.at[1], 1)
        send_part(0, far_center, quarter, 0, False)
        send_part(0, sibling + next_col, col, 0, True)
        with mark("C"):
            pl.semaphore_wait(stage_sem.at[4], 1)
        send_part(0, far_edge, quarter, 0, False)
        send_part(0, here + next_col, col, 0, True)
        s(3)
        f(1)
        s(1)
        f(2)
        s(2)
        h(3)
        h(1)
        h(2)

    video_valid = video_length[0]
    audio_valid = audio_length[0]
    shift = align_offset[0]
    video_rows = arrays[0].shape[0]
    audio_rows = arrays[3].shape[0]
    video_total = n * video_rows
    audio_total = n * audio_rows
    video_reach = video_total // 8
    audio_reach = 5 * audio_total // 8

    def query_places(count, copies, first):
        rows = first + lax.broadcasted_iota(jnp.int32, (count, 1), 0)
        return jnp.concatenate([rows] * copies, axis=0)

    def key_places(count):
        return lax.broadcasted_iota(jnp.int32, (1, count), 1)

    def permit_of(which, copies):
        if which == 0:
            return key_places(video_total) < video_valid
        if which == 1:
            return key_places(audio_total) < audio_valid
        if which == 2:
            where = key_places(audio_total)
            spots = query_places(half * video_rows, copies, side * half * video_rows)
            spots = lax.shift_right_logical(spots, ratio.bit_length() - 1)
            center = jnp.clip(spots + shift, 0, audio_valid - 1)
            return (where < audio_valid) & (jnp.abs(where - center) <= audio_reach)
        return reach_permit(copies, side * half * audio_rows, half * audio_rows, side * (half - margin) * video_rows, (half + margin) * video_rows)

    def reach_permit(copies, query_first, query_count, key_first, key_count):
        where = key_places(key_count) + key_first
        spots = query_places(query_count, copies, query_first)
        center = jnp.clip((spots - shift) * ratio, 0, video_valid - 1)
        return (where < video_valid) & (jnp.abs(where - center) <= video_reach)

    def spread(tokens):
        lane = lax.broadcasted_iota(jnp.int32, tokens.shape, 1) // HDA
        zero = jnp.zeros_like(tokens)
        return jnp.concatenate(
            [jnp.where(lane == head, tokens, zero) for head in range(LANES // HDA)], axis=0
        )

    def fold(stacked):
        rows = stacked.shape[0] // (LANES // HDA)
        merged = jnp.broadcast_to(stacked[:rows], (rows, LANES))
        lane = lax.broadcasted_iota(jnp.int32, merged.shape, 1) // HDA
        for head in range(1, LANES // HDA):
            merged = jnp.where(lane == head, stacked[head * rows : (head + 1) * rows], merged)
        return merged

    def scored(tokens, keys, permit):
        scores = lax.dot_general(
            tokens, keys, (((1,), (1,)), ((), ())), preferred_element_type=jnp.float32
        )
        return jnp.where(permit, scores * (1.0 / math.sqrt(HDA)), -1e30)

    def weighed(scores, peak, permit, values):
        weights = jnp.where(permit, jnp.exp(scores - peak), 0.0)
        total = jnp.sum(weights, axis=1, keepdims=True)
        mixed = jnp.dot(weights.astype(jnp.bfloat16), values, preferred_element_type=jnp.float32)
        return mixed, total

    def tokens_of(ref, first, count, column):
        block = ref[first : first + count, :, column : column + LANES]
        rows = block.shape[1]
        if rows % 16:
            return block.astype(jnp.float32).reshape(count * rows, LANES).astype(block.dtype)
        return block.reshape(count * rows, LANES)

    group3 = GROUPS[3][0]
    heads_each = LANES // HDA

    def host_guests():
        copies = heads_each
        permit = reach_permit(
            copies,
            (half - margin) * audio_rows,
            margin * audio_rows,
            half * video_rows,
            margin * video_rows,
        )
        with mark("WG"):
            pltpu.make_async_copy(guest, guest, recv_sem.at[14]).wait()
            for at in KEYED:
                part = held[at].at[pl.ds(0, margin)]
                pltpu.make_async_copy(part, part, recv_sem.at[12 + KEYED.index(at)]).wait()
        keys, values = held[group3[1]], held[group3[2]]
        rows = margin * audio_rows
        lane = lax.broadcasted_iota(jnp.int32, (rows, LANES), 1)
        packed = jnp.zeros((rows, LANES), jnp.float32)
        for column in range(0, guest.shape[2], LANES):
            tokens = spread(tokens_of(guest, 0, margin, column))
            scores = scored(tokens, tokens_of(keys, margin, margin, column), permit)
            peak = jnp.max(scores, axis=1, keepdims=True).astype(jnp.bfloat16).astype(jnp.float32)
            mixed, total = weighed(scores, peak, permit, tokens_of(values, margin, margin, column))
            coarse = total.astype(jnp.bfloat16).astype(jnp.float32)
            for head in range(copies):
                spot = column // LANES * copies + head
                piece = slice(head * rows, (head + 1) * rows)
                for kind, stat in enumerate((peak, coarse, total - coarse)):
                    packed = jnp.where(lane == 3 * spot + kind, stat[piece], packed)
            part_out[:, :, column : column + LANES] = (
                fold(mixed).reshape(margin, audio_rows, LANES).astype(part_out.dtype)
            )
        part_out[:, :, guest.shape[2] :] = packed.reshape(margin, audio_rows, LANES).astype(
            part_out.dtype
        )
        pltpu.make_async_remote_copy(
            src_ref=part_out,
            dst_ref=part_in,
            send_sem=part_sem.at[0],
            recv_sem=part_sem.at[1],
            device_id={"seq": inner},
            device_id_type=pl.DeviceIdType.MESH,
        ).start()

    def wait_reach():
        for at in group3:
            with mark("W3_%d" % at):
                part = held[at].at[pl.ds(0, half)]
                pltpu.make_async_copy(part, part, recv_sem.at[at]).wait()

    def lower_reach():
        copies = heads_each
        permit = reach_permit(copies, 0, half * audio_rows, 0, half * video_rows)
        wait_reach()
        own = []
        query, keys, values = (held[at] for at in group3)
        for column in range(0, query.shape[2], LANES):
            tokens = spread(tokens_of(query, 0, half, column))
            scores = scored(tokens, tokens_of(keys, 0, half, column), permit)
            peak = jnp.max(scores, axis=1, keepdims=True)
            mixed, total = weighed(scores, peak, permit, tokens_of(values, 0, half, column))
            own.append((fold(mixed), fold(peak), fold(total)))
        with mark("WP"):
            pltpu.make_async_copy(part_in, part_in, part_sem.at[1]).wait()
        first = (half - margin) * audio_rows
        rows = margin * audio_rows
        stats = part_in[:, :, guest.shape[2] :].astype(jnp.float32).reshape(rows, LANES)
        for index, (mixed, peak, total) in enumerate(own):
            column = index * LANES
            theirs = part_in[:, :, column : column + LANES].astype(jnp.float32).reshape(rows, LANES)

            def stat(kind):
                spots = [3 * (index * copies + head) + kind for head in range(copies)]
                return fold(jnp.concatenate([stats[:, spot : spot + 1] for spot in spots], axis=0))

            their_peak = stat(0)
            their_total = stat(1) + stat(2)
            top = jnp.maximum(peak[first:], their_peak)
            mine_factor = jnp.exp(peak[first:] - top)
            their_factor = jnp.exp(their_peak - top)
            joined = mixed[first:] * mine_factor + theirs * their_factor
            joined = joined / (total[first:] * mine_factor + their_total * their_factor)
            whole = jnp.concatenate([mixed[:first] / total[:first], joined], axis=0)
            write_tokens(results[3], column, whole)

    def upper_reach():
        copies = heads_each
        permit = permit_of(3, copies)
        wait_reach()
        query, keys, values = (held[at] for at in group3)
        for column in range(0, query.shape[2], LANES):
            tokens = spread(read_tokens(query, column))
            mixed = softmax_mix(
                tokens,
                read_tokens(keys, column),
                read_tokens(values, column),
                permit,
                1.0 / math.sqrt(HDA),
            )
            write_tokens(results[3], column, fold(mixed))

    def compute(number):
        group, which, halved = GROUPS[number]
        if which == 3:
            pl.when(lower)(lower_reach)
            pl.when(upper)(upper_reach)
            return
        query, keys, values = (held[at] for at in group)
        depth = HDV if which == 0 else HDA
        copies = LANES // depth
        scale = 1.0 / math.sqrt(depth)
        permit = permit_of(which, copies)
        for at in group:
            with mark("W%d_%d" % (which, at)):
                pltpu.make_async_copy(held[at], held[at], recv_sem.at[at]).wait()
        for column in range(0, query.shape[2], LANES):
            tokens = read_tokens(query, column)
            if copies > 1:
                lane = lax.broadcasted_iota(jnp.int32, tokens.shape, 1) // depth
                zero = jnp.zeros_like(tokens)
                tokens = jnp.concatenate(
                    [jnp.where(lane == head, tokens, zero) for head in range(copies)], axis=0
                )
            mixed = softmax_mix(
                tokens, read_tokens(keys, column), read_tokens(values, column), permit, scale
            )
            if copies > 1:
                rows = mixed.shape[0] // copies
                merged = mixed[:rows]
                lane = lax.broadcasted_iota(jnp.int32, merged.shape, 1) // depth
                for head in range(1, copies):
                    merged = jnp.where(lane == head, mixed[head * rows : (head + 1) * rows], merged)
                mixed = merged
            write_tokens(results[which], column, mixed)

    def give_back(number, far=False, close=False):
        group, which, halved = GROUPS[number]
        mine = inner if halved else me
        target = outs[which].at[:, columns(results[which].shape[2], mine)]

        def give(block, peer):
            pltpu.make_async_remote_copy(
                src_ref=results[which].at[block],
                dst_ref=target,
                send_sem=back_send.at[which],
                recv_sem=back_recv.at[which],
                device_id={"seq": peer},
                device_id_type=pl.DeviceIdType.MESH,
            ).start()

        if far:

            @pl.loop(0, half)
            def _(step):
                peer = (1 - side) * half + step
                give(peer, peer)

        if not close:
            return

        @pl.loop(1, half)
        def _(step):
            block = lax.rem(inner + step, half)
            peer = side * half + block
            give(block if halved else peer, peer)

        pltpu.make_async_copy(results[which].at[mine], target, back_recv.at[which]).start()

    compute(0)
    give_back(0, close=True)
    pl.when(central)(lambda: give_back(0, far=True))
    pl.when(upper)(host_guests)
    compute(1)
    give_back(1, close=True)
    pl.when(central)(lambda: give_back(1, far=True))
    pl.when(jnp.logical_not(central) & upper)(lambda: give_back(0, far=True))
    pl.when(jnp.logical_not(central) & upper)(lambda: give_back(1, far=True))
    compute(2)
    give_back(2, far=False, close=True)
    compute(3)
    pl.when(jnp.logical_not(central) & (side == 0))(lambda: give_back(0, far=True))
    pl.when(jnp.logical_not(central) & (side == 0))(lambda: give_back(1, far=True))
    give_back(3, far=False, close=True)

    def wait_bytes(ref, blocks, sem):
        part = ref.at[pl.ds(0, blocks)]
        pltpu.make_async_copy(part, part, sem).wait()

    for group, which, halved in GROUPS:
        for at in group:
            wait_bytes(held[at], half - 1, send_sem.at[at])
            if not halved or (which == 2 and at != group[0]):
                wait_bytes(held[at], half, far_sem.at[at])
            elif which == 3:

                @pl.when(hosted)
                def _(at=at):
                    wait_bytes(held[at], half, far_sem.at[at])

    @pl.when(upper)
    def _():
        pltpu.make_async_copy(part_out, part_out, part_sem.at[0]).wait()

    for which in range(4):
        with mark("R%d" % which):
            pltpu.make_async_copy(outs[which], outs[which], back_recv.at[which]).wait()

    for which in range(4):
        wait_bytes(results[which], results[which].shape[0] - 1, back_send.at[which])


def write_out(*refs):
    sources, targets, sem = refs[:4], refs[4:8], refs[8]
    copies = [pltpu.make_async_copy(*pair, sem.at[at]) for at, pair in enumerate(zip(sources, targets))]
    for copy in copies:
        copy.start()
    for copy in copies:
        copy.wait()


def fused_shards(*arguments):
    n = lax.axis_size("seq")
    arrays = arguments[:12]
    lengths = arguments[12:]
    arrays = [pltpu.with_memory_space_constraint(a, pltpu.HBM) for a in arrays]
    ratio = arrays[0].shape[0] // arrays[3].shape[0]
    held = [pltpu.VMEM(s, a.dtype) for s, a in zip(held_shapes(n, arrays), arrays)]
    guest_blocks = held[7].shape[0] - n // 2
    guest_rows, guest_width = held[9].shape[1:]
    guests = [
        pltpu.VMEM((guest_blocks, guest_rows, guest_width), jnp.bfloat16),
        pltpu.VMEM((guest_blocks, guest_rows, guest_width + LANES), jnp.bfloat16),
        pltpu.VMEM((guest_blocks, guest_rows, guest_width + LANES), jnp.bfloat16),
    ]
    results = [
        pltpu.VMEM((n, *held[0].shape[1:]), jnp.bfloat16),
        pltpu.VMEM((n, *held[3].shape[1:]), jnp.bfloat16),
        pltpu.VMEM((n // 2, *held[6].shape[1:]), jnp.bfloat16),
        pltpu.VMEM((n // 2, *held[9].shape[1:]), jnp.bfloat16),
    ]
    shapes = [arrays[at].shape for at in (0, 3, 6, 9)]
    anywhere = pl.BlockSpec(memory_space=pl.ANY)
    scalars = pl.BlockSpec(memory_space=pltpu.SMEM)
    vectors = pl.BlockSpec(memory_space=pltpu.VMEM)
    mixed = pl.pallas_call(
        functools.partial(fused_kernel, n, ratio),
        out_shape=tuple(pltpu.VMEM(shape, jnp.bfloat16) for shape in shapes),
        in_specs=[scalars] * 3 + [pl.BlockSpec(memory_space=pltpu.HBM)] * 12,
        out_specs=(vectors,) * 4,
        scratch_shapes=held
        + results
        + [
            pltpu.SemaphoreType.DMA((12,)),
            pltpu.SemaphoreType.DMA((12,)),
            pltpu.SemaphoreType.DMA((15,)),
            pltpu.SemaphoreType.DMA((4,)),
            pltpu.SemaphoreType.DMA((4,)),
            pltpu.SemaphoreType.REGULAR((6,)),
            pltpu.SemaphoreType.DMA((2,)),
            *guests,
        ],
        compiler_params=pltpu.CompilerParams(
            collective_id=0, has_side_effects=True, vmem_limit_bytes=24 * 2**20
        ),
    )(*lengths, *arrays)
    return pl.pallas_call(
        write_out,
        out_shape=tuple(jax.ShapeDtypeStruct(shape, jnp.bfloat16) for shape in shapes),
        in_specs=[vectors] * 4,
        out_specs=(anywhere,) * 4,
        scratch_shapes=[pltpu.SemaphoreType.DMA((4,))],
        compiler_params=pltpu.CompilerParams(vmem_limit_bytes=2**20),
    )(*mixed)


def kernel_fits(n, video_rows, audio_rows):
    if n % 16 or HV % n or HA % n or (HV // n * HDV) % LANES or (HA // n * HDA) % LANES:
        return False
    ratio = video_rows // audio_rows
    return video_rows == ratio * audio_rows and ratio & (ratio - 1) == 0 and n * audio_rows % 16 == 0 and audio_rows % 8 == 0


def dispatch(*arguments):
    fits = kernel_fits(lax.axis_size("seq"), arguments[0].shape[0], arguments[3].shape[0])
    return (fused_shards if fits else shards)(*arguments)


def solution(mesh):
    placed = (
        P(("clip", "seq"), None),
        P(("clip", "seq"), None),
        P(("clip", "seq"), None),
        P(("clip", "seq"), None),
        P(("clip", "seq"), None),
        P(("clip", "seq"), None),
        P(("clip", "seq"), None),
        P(("clip", "seq"), None),
        P(("clip", "seq"), None),
        P(("clip", "seq"), None),
        P(("clip", "seq"), None),
        P(("clip", "seq"), None),
        P("clip"),
        P("clip"),
        P("clip"),
    )
    return jax.shard_map(
        dispatch,
        mesh=mesh,
        in_specs=placed,
        out_specs=(
            P(("clip", "seq"), None),
            P(("clip", "seq"), None),
            P(("clip", "seq"), None),
            P(("clip", "seq"), None),
        ),
        check_vma=False,
    )
```

```python
import contextlib
import functools
import math

import jax
import jax.numpy as jnp
from jax import lax
from jax.experimental import pallas as pl
from jax.experimental.pallas import tpu as pltpu
from jax.sharding import PartitionSpec as P

HV = 32
HDV = 128
HA = 32
HDA = 64


def block_size(total, limit):
    chosen = min(total, limit)
    while total % chosen:
        chosen -= 1
    return chosen


def split_heads(tokens, heads, depth, copies):
    rows = tokens.shape[0]
    shaped = tokens.reshape(copies, rows // copies, heads, depth).transpose(2, 0, 1, 3)
    return shaped.reshape(heads * copies, rows // copies, depth)


def spread_heads(tokens, heads, depth, copies):
    rows = tokens.shape[0]
    shaped = tokens.reshape(rows, heads, depth).transpose(1, 0, 2)
    shaped = jnp.broadcast_to(shaped[:, None], (heads, copies, rows, depth))
    return shaped.reshape(heads * copies, rows, depth)


def join_heads(owned, heads, depth, copies):
    part_rows = owned.shape[1]
    shaped = owned.reshape(heads, copies, part_rows, depth).transpose(1, 2, 0, 3)
    return shaped.reshape(copies * part_rows, heads * depth)


def owned_positions(rows, copies, devices, index):
    part_rows = rows // copies
    flat = jnp.arange(devices * part_rows, dtype=jnp.int32)
    return flat // part_rows * rows + index % copies * part_rows + flat % part_rows


def online_update(carry, scores, permit, value_tile, value_form):
    running, total, accum = carry
    scores = jnp.where(permit, scores, -1e30)
    newmax = jnp.maximum(running, jnp.max(scores, axis=2))
    weights = jnp.where(permit, jnp.exp(scores - newmax[:, :, None]), 0.0)
    factor = jnp.exp(running - newmax)
    total = total * factor + jnp.sum(weights, axis=2)
    mixed = jnp.einsum(
        value_form, weights.astype(jnp.bfloat16), value_tile, preferred_element_type=jnp.float32
    )
    accum = accum * factor[:, :, None] + mixed
    return (newmax, total, accum)


def fold_initial(rows, heads, depth):
    return (
        jnp.full((heads, rows), -1e30, jnp.float32),
        jnp.zeros((heads, rows), jnp.float32),
        jnp.zeros((heads, rows, depth), jnp.float32),
    )


def fold_piece(carry, local_query, key_rows, value_rows, permit, heads, depth):
    keyed = key_rows.reshape(key_rows.shape[0], heads, depth)
    valued = value_rows.reshape(value_rows.shape[0], heads, depth)
    scores = jnp.einsum("qhd,khd->hqk", local_query, keyed, preferred_element_type=jnp.float32) * (
        1.0 / math.sqrt(depth)
    )
    return online_update(carry, scores, permit[None], valued, "hqk,khd->hqd")


def fold_finish(carry, heads, depth):
    running, total, accum = carry
    result = (accum / total[:, :, None]).astype(jnp.bfloat16)
    return result.transpose(1, 0, 2).reshape(result.shape[1], heads * depth)


def attend_local(queries, keys, values, query_pos, key_pos, allowed):
    heads, q_count, depth = queries.shape
    k_count = keys.shape[1]
    q_block = block_size(q_count, 512)
    k_block = block_size(k_count, 2048)
    scale = 1.0 / math.sqrt(depth)
    q_tiles = queries.reshape(heads, q_count // q_block, q_block, depth).transpose(1, 0, 2, 3)
    k_tiles = keys.reshape(heads, k_count // k_block, k_block, depth).transpose(1, 0, 2, 3)
    v_tiles = values.reshape(heads, k_count // k_block, k_block, depth).transpose(1, 0, 2, 3)
    q_places = query_pos.reshape(q_count // q_block, q_block)
    k_places = key_pos.reshape(k_count // k_block, k_block)

    def one_tile(packed):
        q_tile, q_where = packed

        def absorb(carry, piece):
            k_tile, v_tile, k_where = piece
            scores = (
                jnp.einsum("hqd,hkd->hqk", q_tile, k_tile, preferred_element_type=jnp.float32)
                * scale
            )
            permit = allowed(q_where[:, None], k_where[None, :])[None]
            return (online_update(carry, scores, permit, v_tile, "hqk,hkd->hqd"), None)

        initial = fold_initial(q_block, heads, depth)
        final_state, unused = lax.scan(absorb, initial, (k_tiles, v_tiles, k_places))
        running, total, accum = final_state
        return (accum / total[:, :, None]).astype(jnp.bfloat16)

    tiles = lax.map(one_tile, (q_tiles, q_places))
    return tiles.transpose(1, 0, 2, 3).reshape(heads, q_count, depth)


def shards(
    video_query,
    video_keys,
    video_values,
    audio_query,
    audio_keys,
    audio_values,
    cross_video_query,
    cross_video_keys,
    cross_video_values,
    cross_audio_query,
    cross_audio_keys,
    cross_audio_values,
    video_length,
    audio_length,
    align_offset,
):
    devices = lax.axis_size("seq")
    index = lax.axis_index("seq")
    video_rows = video_query.shape[0]
    audio_rows = audio_query.shape[0]
    video_total = video_rows * devices
    audio_total = audio_rows * devices
    video_reach = video_total // 8
    audio_reach = 5 * audio_total // 8
    video_valid = video_length[0]
    audio_valid = audio_length[0]
    align_shift = align_offset[0]
    copies = max(devices // HV, 1)
    video_places = jnp.arange(video_total, dtype=jnp.int32)
    audio_places = jnp.arange(audio_total, dtype=jnp.int32)

    def video_open(q_where, k_where):
        return k_where < video_valid

    def toward_video(q_where, k_where):
        center = jnp.clip(q_where * audio_total // video_total + align_shift, 0, audio_valid - 1)
        return (k_where < audio_valid) & (jnp.abs(k_where - center) <= audio_reach)

    def toward_audio(q_where, k_where):
        center = jnp.clip((q_where - align_shift) * video_total // audio_total, 0, video_valid - 1)
        return (k_where < video_valid) & (jnp.abs(k_where - center) <= video_reach)

    video_owned = (
        lax.all_to_all(
            split_heads(video_query, HV, HDV, copies),
            "seq",
            split_axis=0,
            concat_axis=1,
            tiled=True,
        ),
        lax.all_to_all(
            spread_heads(video_keys, HV, HDV, copies),
            "seq",
            split_axis=0,
            concat_axis=1,
            tiled=True,
        ),
        lax.all_to_all(
            spread_heads(video_values, HV, HDV, copies),
            "seq",
            split_axis=0,
            concat_axis=1,
            tiled=True,
        ),
    )
    video_done = attend_local(
        video_owned[0],
        video_owned[1],
        video_owned[2],
        owned_positions(video_rows, copies, devices, index),
        video_places,
        video_open,
    )
    video_mixed = join_heads(
        lax.all_to_all(video_done, "seq", split_axis=1, concat_axis=0, tiled=True), HV, HDV, copies
    )
    audio_local = audio_query.reshape(audio_rows, HA, HDA)
    piece = (
        lax.all_gather(audio_keys, "seq", axis=0, tiled=True),
        lax.all_gather(audio_values, "seq", axis=0, tiled=True),
    )
    k_where = jnp.arange(piece[0].shape[0], dtype=jnp.int32)
    audio_k_where = k_where[None, :]
    permit = audio_k_where < audio_valid
    audio_state = fold_piece(
        fold_initial(audio_rows, HA, HDA), audio_local, piece[0], piece[1], permit, HA, HDA
    )
    audio_mixed = fold_finish(audio_state, HA, HDA)
    cross_owned = (
        lax.all_to_all(
            split_heads(cross_video_query, HA, HDA, copies),
            "seq",
            split_axis=0,
            concat_axis=1,
            tiled=True,
        ),
        lax.all_to_all(
            spread_heads(cross_audio_keys, HA, HDA, copies),
            "seq",
            split_axis=0,
            concat_axis=1,
            tiled=True,
        ),
        lax.all_to_all(
            spread_heads(cross_audio_values, HA, HDA, copies),
            "seq",
            split_axis=0,
            concat_axis=1,
            tiled=True,
        ),
    )
    cross_done = attend_local(
        cross_owned[0],
        cross_owned[1],
        cross_owned[2],
        owned_positions(video_rows, copies, devices, index),
        audio_places,
        toward_video,
    )
    video_cross = join_heads(
        lax.all_to_all(cross_done, "seq", split_axis=1, concat_axis=0, tiled=True), HA, HDA, copies
    )
    listen_owned = (
        lax.all_to_all(
            split_heads(cross_audio_query, HA, HDA, copies),
            "seq",
            split_axis=0,
            concat_axis=1,
            tiled=True,
        ),
        lax.all_to_all(
            spread_heads(cross_video_keys, HA, HDA, copies),
            "seq",
            split_axis=0,
            concat_axis=1,
            tiled=True,
        ),
        lax.all_to_all(
            spread_heads(cross_video_values, HA, HDA, copies),
            "seq",
            split_axis=0,
            concat_axis=1,
            tiled=True,
        ),
    )
    listen_done = attend_local(
        listen_owned[0],
        listen_owned[1],
        listen_owned[2],
        owned_positions(audio_rows, copies, devices, index),
        video_places,
        toward_audio,
    )
    audio_cross = join_heads(
        lax.all_to_all(listen_done, "seq", split_axis=1, concat_axis=0, tiled=True), HA, HDA, copies
    )
    return (video_mixed, audio_mixed, video_cross, audio_cross)


LANES = 128
mark = lambda name: contextlib.nullcontext()
KEYED = (7, 8)
PARTIAL = 3

GROUPS = (
    ((0, 1, 2), 0, False),
    ((3, 4, 5), 1, False),
    ((6, 10, 11), 2, True),
    ((9, 7, 8), 3, True),
)


def softmax_mix(query, keys, values, permit, scale):
    scores = lax.dot_general(
        query, keys, (((1,), (1,)), ((), ())), preferred_element_type=jnp.float32
    )
    scores = jnp.where(permit, scores * scale, -1e30)
    peak = jnp.max(scores, axis=1, keepdims=True)
    weights = jnp.exp(scores - peak)
    total = jnp.sum(weights, axis=1, keepdims=True)
    mixed = jnp.dot(weights.astype(jnp.bfloat16), values, preferred_element_type=jnp.float32)
    return mixed / total


def read_tokens(ref, column):
    block = ref[:, :, column : column + LANES]
    n, rows, _ = block.shape
    if rows % 16:
        return block.astype(jnp.float32).reshape(n * rows, LANES).astype(block.dtype)
    return block.reshape(n * rows, LANES)


def write_tokens(ref, column, result):
    n, rows, _ = ref.shape
    ref[:, :, column : column + LANES] = result.reshape(n, rows, LANES).astype(ref.dtype)


def margin_blocks(n, video_rows):
    return min(-(-(3 * n * video_rows // 16) // video_rows), n // 2)


def held_shapes(n, arrays):
    half = n // 2
    shapes = [None] * 12
    for group, which, halved in GROUPS:
        for place, at in enumerate(group):
            rows, cols = arrays[at].shape
            blocks = n
            if halved and place == 0:
                blocks = half
            elif which == 3:
                blocks = half + margin_blocks(n, rows)
            shapes[at] = (blocks, rows, cols // (half if halved else n))
    return shapes


def fused_kernel(n, ratio, *refs):
    video_length, audio_length, align_offset = refs[:3]
    arrays = refs[3:15]
    outs = refs[15:19]
    held = refs[19:31]
    results = refs[31:35]
    send_sem, far_sem, recv_sem, back_send, back_recv, stage_sem, part_sem, guest, part_out, part_in = refs[
        35:
    ]
    half = n // 2
    quarter = n // 4
    margin = held[7].shape[0] - half
    me = lax.axis_index("seq")
    side = me // half
    inner = lax.rem(me, half)
    near = (me >= half - margin) & (me < half + margin)
    lower = side == 0
    upper = side == 1
    hosted = near & lower
    edge_key = near & upper

    def arrival(at, same):
        if at in KEYED and same:
            return recv_sem.at[jnp.where(edge_key, 12 + KEYED.index(at), at)]
        return recv_sem.at[at]

    def columns(width, owner):
        return pl.ds(pl.multiple_of(owner * width, LANES), width)

    def slot_of(group, which, halved, at, to_side):
        if halved and at == group[0]:
            return inner
        if which == 3:
            return me - to_side * (half - margin)
        return me

    def send(at, owner, slot, peer, sem, same):
        pltpu.make_async_remote_copy(
            src_ref=arrays[at].at[:, columns(held[at].shape[2], owner)],
            dst_ref=held[at].at[slot],
            send_sem=sem.at[at],
            recv_sem=arrival(at, same),
            device_id={"seq": peer},
            device_id_type=pl.DeviceIdType.MESH,
        ).start()

    for group, which, halved in GROUPS:
        for at in group:
            pltpu.make_async_copy(
                arrays[at].at[:, columns(held[at].shape[2], inner if halved else me)],
                held[at].at[slot_of(group, which, halved, at, side)],
                arrival(at, True),
            ).start()

    col = quarter // 2
    level = me // quarter
    rank = lax.rem(me, quarter)
    core = lax.rem(rank, col)
    mine_col = rank - core
    next_col = col - mine_col
    central = (level == 1) | (level == 2)
    here = level * quarter
    sibling = (level + 1 - 2 * lax.rem(level, 2)) * quarter
    far_center = (2 - side) * quarter
    far_edge = (3 - 3 * side) * quarter

    barrier = pltpu.get_barrier_semaphore()

    def signal(sem, peer):
        pl.semaphore_signal(
            sem, inc=1, device_id={"seq": peer}, device_id_type=pl.DeviceIdType.MESH
        )

    def greet(base, first):
        @pl.loop(first, col)
        def _(step):
            signal(barrier, base + lax.rem(core + step, col))

    @pl.when(central)
    def _():
        greet(far_center + mine_col, 0)

    greet(here + mine_col, 1)

    @pl.when(central)
    def _():
        greet(here + next_col, 0)
        greet(sibling + mine_col, 0)

    with mark("BAR"):
        pl.semaphore_wait(barrier, jnp.where(central, 3 * col - 1, 2 * col - 1))

    def send_part(number, base, count, first, same):
        group, which, halved = GROUPS[number]
        spot = core if count == col else rank

        def sends():
            @pl.loop(first, count)
            def _(step):
                peer = base + lax.rem(spot + step, count)
                owner = lax.rem(peer, half) if halved else peer
                for at in group:
                    if halved and at == group[0] and not same:
                        continue
                    slot = slot_of(group, which, halved, at, side if same else 1 - side)
                    send(at, owner, slot, peer, send_sem if same else far_sem, same)

        if which == 3 and not same:
            pl.when(hosted)(sends)
        else:
            sends()

    def f(number):
        send_part(number, far_edge, quarter, 0, False)
        send_part(number, far_center, quarter, 0, False)

    def k(number):
        send_part(number, far_center, quarter, 0, False)

    def g(number):
        send_part(number, far_edge, quarter, 0, False)

    def s(number):
        send_part(number, sibling, quarter, 0, True)

    def v(number):
        group = GROUPS[number][0]

        @pl.when(hosted)
        def _():
            @pl.loop(0, half)
            def _(step):
                owner = lax.rem(inner + step, half)
                pltpu.make_async_remote_copy(
                    src_ref=arrays[group[0]].at[:, columns(held[group[0]].shape[2], owner)],
                    dst_ref=guest.at[me - (half - margin)],
                    send_sem=far_sem.at[group[0]],
                    recv_sem=recv_sem.at[14],
                    device_id={"seq": half + owner},
                    device_id_type=pl.DeviceIdType.MESH,
                ).start()

    def h(number):
        send_part(number, here, quarter, 1, True)

    across = rank + next_col - mine_col

    @pl.when(central & lower)
    def _():
        signal(stage_sem.at[0], here + across)
        send_part(0, far_center + mine_col, col, 0, False)
        h(0)
        with mark("Y"):
            pl.semaphore_wait(stage_sem.at[0], 1)
        send_part(0, far_center + next_col, col, 0, False)
        with mark("O"):
            pl.semaphore_wait(stage_sem.at[2], 1)
        signal(stage_sem.at[1], sibling + rank)
        signal(stage_sem.at[5], here + across)
        with mark("Y2"):
            pl.semaphore_wait(stage_sem.at[5], 1)
        signal(stage_sem.at[3], far_center + rank)
        s(0)
        with mark("B"):
            pl.semaphore_wait(stage_sem.at[3], 1)
        signal(stage_sem.at[4], sibling + rank)
        g(0)
        v(3)
        g(1)
        k(1)
        g(3)
        k(3)
        g(2)
        k(2)
        h(3)
        s(3)
        h(1)
        s(1)
        h(2)
        s(2)

    @pl.when(central & upper)
    def _():
        signal(stage_sem.at[0], here + across)
        send_part(0, far_center + mine_col, col, 0, False)
        h(0)
        with mark("Y"):
            pl.semaphore_wait(stage_sem.at[0], 1)
        send_part(0, far_center + next_col, col, 0, False)
        with mark("O"):
            pl.semaphore_wait(stage_sem.at[2], 1)
        signal(stage_sem.at[1], sibling + rank)
        signal(stage_sem.at[5], here + across)
        with mark("Y2"):
            pl.semaphore_wait(stage_sem.at[5], 1)
        signal(stage_sem.at[3], far_center + rank)
        s(0)
        with mark("B"):
            pl.semaphore_wait(stage_sem.at[3], 1)
        signal(stage_sem.at[4], sibling + rank)
        g(0)
        g(1)
        k(1)
        g(2)
        k(2)
        h(3)
        s(3)
        h(1)
        s(1)
        h(2)
        s(2)

    @pl.when(jnp.logical_not(central))
    def _():
        signal(stage_sem.at[2], sibling + rank)
        send_part(0, sibling + mine_col, col, 0, True)
        send_part(0, here + mine_col, col, 1, True)
        with mark("A"):
            pl.semaphore_wait(stage_sem.at[1], 1)
        k(0)
        send_part(0, sibling + next_col, col, 0, True)
        with mark("C"):
            pl.semaphore_wait(stage_sem.at[4], 1)
        g(0)
        send_part(0, here + next_col, col, 0, True)
        s(3)
        g(1)
        k(1)
        s(1)
        g(2)
        k(2)
        s(2)
        h(3)
        h(1)
        h(2)

    video_valid = video_length[0]
    audio_valid = audio_length[0]
    shift = align_offset[0]
    video_rows = arrays[0].shape[0]
    audio_rows = arrays[3].shape[0]
    video_total = n * video_rows
    audio_total = n * audio_rows
    video_reach = video_total // 8
    audio_reach = 5 * audio_total // 8

    def query_places(count, copies, first):
        rows = first + lax.broadcasted_iota(jnp.int32, (count, 1), 0)
        return jnp.concatenate([rows] * copies, axis=0)

    def key_places(count):
        return lax.broadcasted_iota(jnp.int32, (1, count), 1)

    def permit_of(which, copies):
        if which == 0:
            return key_places(video_total) < video_valid
        if which == 1:
            return key_places(audio_total) < audio_valid
        if which == 2:
            where = key_places(audio_total)
            spots = query_places(half * video_rows, copies, side * half * video_rows)
            spots = lax.shift_right_logical(spots, ratio.bit_length() - 1)
            center = jnp.clip(spots + shift, 0, audio_valid - 1)
            return (where < audio_valid) & (jnp.abs(where - center) <= audio_reach)
        return reach_permit(copies, side * half * audio_rows, half * audio_rows, side * (half - margin) * video_rows, (half + margin) * video_rows)

    def reach_permit(copies, query_first, query_count, key_first, key_count):
        where = key_places(key_count) + key_first
        spots = query_places(query_count, copies, query_first)
        center = jnp.clip((spots - shift) * ratio, 0, video_valid - 1)
        return (where < video_valid) & (jnp.abs(where - center) <= video_reach)

    def spread(tokens):
        lane = lax.broadcasted_iota(jnp.int32, tokens.shape, 1) // HDA
        zero = jnp.zeros_like(tokens)
        return jnp.concatenate(
            [jnp.where(lane == head, tokens, zero) for head in range(LANES // HDA)], axis=0
        )

    def fold(stacked):
        rows = stacked.shape[0] // (LANES // HDA)
        merged = jnp.broadcast_to(stacked[:rows], (rows, LANES))
        lane = lax.broadcasted_iota(jnp.int32, merged.shape, 1) // HDA
        for head in range(1, LANES // HDA):
            merged = jnp.where(lane == head, stacked[head * rows : (head + 1) * rows], merged)
        return merged

    def scored(tokens, keys, permit):
        scores = lax.dot_general(
            tokens, keys, (((1,), (1,)), ((), ())), preferred_element_type=jnp.float32
        )
        return jnp.where(permit, scores * (1.0 / math.sqrt(HDA)), -1e30)

    def weighed(scores, peak, permit, values):
        weights = jnp.where(permit, jnp.exp(scores - peak), 0.0)
        total = jnp.sum(weights, axis=1, keepdims=True)
        mixed = jnp.dot(weights.astype(jnp.bfloat16), values, preferred_element_type=jnp.float32)
        return mixed, total

    def tokens_of(ref, first, count, column):
        block = ref[first : first + count, :, column : column + LANES]
        rows = block.shape[1]
        if rows % 16:
            return block.astype(jnp.float32).reshape(count * rows, LANES).astype(block.dtype)
        return block.reshape(count * rows, LANES)

    group3 = GROUPS[3][0]
    heads_each = LANES // HDA

    def host_guests():
        copies = heads_each
        permit = reach_permit(
            copies,
            (half - margin) * audio_rows,
            margin * audio_rows,
            half * video_rows,
            margin * video_rows,
        )
        with mark("WG"):
            pltpu.make_async_copy(guest, guest, recv_sem.at[14]).wait()
            for at in KEYED:
                part = held[at].at[pl.ds(0, margin)]
                pltpu.make_async_copy(part, part, recv_sem.at[12 + KEYED.index(at)]).wait()
        keys, values = held[group3[1]], held[group3[2]]
        rows = margin * audio_rows
        lane = lax.broadcasted_iota(jnp.int32, (rows, LANES), 1)
        packed = jnp.zeros((rows, LANES), jnp.float32)
        for column in range(0, guest.shape[2], LANES):
            tokens = spread(tokens_of(guest, 0, margin, column))
            scores = scored(tokens, tokens_of(keys, margin, margin, column), permit)
            peak = jnp.max(scores, axis=1, keepdims=True).astype(jnp.bfloat16).astype(jnp.float32)
            mixed, total = weighed(scores, peak, permit, tokens_of(values, margin, margin, column))
            coarse = total.astype(jnp.bfloat16).astype(jnp.float32)
            for head in range(copies):
                spot = column // LANES * copies + head
                piece = slice(head * rows, (head + 1) * rows)
                for kind, stat in enumerate((peak, coarse, total - coarse)):
                    packed = jnp.where(lane == 3 * spot + kind, stat[piece], packed)
            part_out[:, :, column : column + LANES] = (
                fold(mixed).reshape(margin, audio_rows, LANES).astype(part_out.dtype)
            )
        part_out[:, :, guest.shape[2] :] = packed.reshape(margin, audio_rows, LANES).astype(
            part_out.dtype
        )
        pltpu.make_async_remote_copy(
            src_ref=part_out,
            dst_ref=part_in,
            send_sem=part_sem.at[0],
            recv_sem=part_sem.at[1],
            device_id={"seq": inner},
            device_id_type=pl.DeviceIdType.MESH,
        ).start()

    def wait_reach():
        for at in group3:
            with mark("W3_%d" % at):
                part = held[at].at[pl.ds(0, half)]
                pltpu.make_async_copy(part, part, recv_sem.at[at]).wait()

    def lower_reach():
        copies = heads_each
        permit = reach_permit(copies, 0, half * audio_rows, 0, half * video_rows)
        wait_reach()
        own = []
        query, keys, values = (held[at] for at in group3)
        for column in range(0, query.shape[2], LANES):
            tokens = spread(tokens_of(query, 0, half, column))
            scores = scored(tokens, tokens_of(keys, 0, half, column), permit)
            peak = jnp.max(scores, axis=1, keepdims=True)
            mixed, total = weighed(scores, peak, permit, tokens_of(values, 0, half, column))
            own.append((fold(mixed), fold(peak), fold(total)))
        with mark("WP"):
            pltpu.make_async_copy(part_in, part_in, part_sem.at[1]).wait()
        first = (half - margin) * audio_rows
        rows = margin * audio_rows
        stats = part_in[:, :, guest.shape[2] :].astype(jnp.float32).reshape(rows, LANES)
        for index, (mixed, peak, total) in enumerate(own):
            column = index * LANES
            theirs = part_in[:, :, column : column + LANES].astype(jnp.float32).reshape(rows, LANES)

            def stat(kind):
                spots = [3 * (index * copies + head) + kind for head in range(copies)]
                return fold(jnp.concatenate([stats[:, spot : spot + 1] for spot in spots], axis=0))

            their_peak = stat(0)
            their_total = stat(1) + stat(2)
            top = jnp.maximum(peak[first:], their_peak)
            mine_factor = jnp.exp(peak[first:] - top)
            their_factor = jnp.exp(their_peak - top)
            joined = mixed[first:] * mine_factor + theirs * their_factor
            joined = joined / (total[first:] * mine_factor + their_total * their_factor)
            whole = jnp.concatenate([mixed[:first] / total[:first], joined], axis=0)
            write_tokens(results[3], column, whole)

    def upper_reach():
        copies = heads_each
        permit = permit_of(3, copies)
        wait_reach()
        query, keys, values = (held[at] for at in group3)
        for column in range(0, query.shape[2], LANES):
            tokens = spread(read_tokens(query, column))
            mixed = softmax_mix(
                tokens,
                read_tokens(keys, column),
                read_tokens(values, column),
                permit,
                1.0 / math.sqrt(HDA),
            )
            write_tokens(results[3], column, fold(mixed))

    def compute(number, low=None):
        group, which, halved = GROUPS[number]
        if which == 3:
            (lower_reach if low else upper_reach)()
            return
        query, keys, values = (held[at] for at in group)
        depth = HDV if which == 0 else HDA
        copies = LANES // depth
        scale = 1.0 / math.sqrt(depth)
        permit = permit_of(which, copies)
        for at in group:
            with mark("W%d_%d" % (which, at)):
                pltpu.make_async_copy(held[at], held[at], recv_sem.at[at]).wait()
        for column in range(0, query.shape[2], LANES):
            tokens = read_tokens(query, column)
            if copies > 1:
                lane = lax.broadcasted_iota(jnp.int32, tokens.shape, 1) // depth
                zero = jnp.zeros_like(tokens)
                tokens = jnp.concatenate(
                    [jnp.where(lane == head, tokens, zero) for head in range(copies)], axis=0
                )
            mixed = softmax_mix(
                tokens, read_tokens(keys, column), read_tokens(values, column), permit, scale
            )
            if copies > 1:
                rows = mixed.shape[0] // copies
                merged = mixed[:rows]
                lane = lax.broadcasted_iota(jnp.int32, merged.shape, 1) // depth
                for head in range(1, copies):
                    merged = jnp.where(lane == head, mixed[head * rows : (head + 1) * rows], merged)
                mixed = merged
            write_tokens(results[which], column, mixed)

    def far_range(far):
        return {1: (0, half), 2: (0, col), 3: (col, half)}[int(far)]

    def give_back(number, far=False, close=False):
        group, which, halved = GROUPS[number]
        mine = inner if halved else me
        target = outs[which].at[:, columns(results[which].shape[2], mine)]

        def give(block, peer):
            pltpu.make_async_remote_copy(
                src_ref=results[which].at[block],
                dst_ref=target,
                send_sem=back_send.at[which],
                recv_sem=back_recv.at[which],
                device_id={"seq": peer},
                device_id_type=pl.DeviceIdType.MESH,
            ).start()

        if far:

            @pl.loop(*far_range(far))
            def _(step):
                peer = (1 - side) * half + step
                give(peer, peer)

        if not close:
            return

        @pl.loop(1, half)
        def _(step):
            block = lax.rem(inner + step, half)
            peer = side * half + block
            give(block if halved else peer, peer)

        pltpu.make_async_copy(results[which].at[mine], target, back_recv.at[which]).start()

    @pl.when(lower)
    def _():
        compute(0)
        give_back(0, close=True)
        pl.when(central)(lambda: give_back(0, far=1))
        compute(1)
        give_back(1, close=True)
        pl.when(central)(lambda: give_back(1, far=1))
        compute(2)
        give_back(2, far=False, close=True)
        compute(3, True)
        pl.when(jnp.logical_not(central))(lambda: give_back(0, far=1))
        pl.when(jnp.logical_not(central))(lambda: give_back(1, far=1))
        give_back(3, far=False, close=True)

    @pl.when(upper)
    def _():
        compute(0)
        give_back(0, close=True)
        pl.when(central)(lambda: give_back(0, far=2))
        pl.when(central)(lambda: give_back(0, far=3))
        host_guests()
        compute(1)
        give_back(1, close=True)
        pl.when(central)(lambda: give_back(1, far=2))
        pl.when(central)(lambda: give_back(1, far=3))
        pl.when(jnp.logical_not(central))(lambda: give_back(0, far=2))
        pl.when(jnp.logical_not(central))(lambda: give_back(1, far=2))
        pl.when(jnp.logical_not(central))(lambda: give_back(0, far=3))
        pl.when(jnp.logical_not(central))(lambda: give_back(1, far=3))
        compute(2)
        give_back(2, far=False, close=True)
        compute(3, False)
        give_back(3, far=False, close=True)


    def wait_bytes(ref, blocks, sem):
        part = ref.at[pl.ds(0, blocks)]
        pltpu.make_async_copy(part, part, sem).wait()

    for group, which, halved in GROUPS:
        for at in group:
            wait_bytes(held[at], half - 1, send_sem.at[at])
            if not halved or (which == 2 and at != group[0]):
                wait_bytes(held[at], half, far_sem.at[at])
            elif which == 3:

                @pl.when(hosted)
                def _(at=at):
                    wait_bytes(held[at], half, far_sem.at[at])

    @pl.when(upper)
    def _():
        pltpu.make_async_copy(part_out, part_out, part_sem.at[0]).wait()

    for which in range(4):
        with mark("R%d" % which):
            pltpu.make_async_copy(outs[which], outs[which], back_recv.at[which]).wait()

    for which in range(4):
        wait_bytes(results[which], results[which].shape[0] - 1, back_send.at[which])


def write_out(*refs):
    sources, targets, sem = refs[:4], refs[4:8], refs[8]
    copies = [pltpu.make_async_copy(*pair, sem.at[at]) for at, pair in enumerate(zip(sources, targets))]
    for copy in copies:
        copy.start()
    for copy in copies:
        copy.wait()


def fused_shards(*arguments):
    n = lax.axis_size("seq")
    arrays = arguments[:12]
    lengths = arguments[12:]
    arrays = [pltpu.with_memory_space_constraint(a, pltpu.HBM) for a in arrays]
    ratio = arrays[0].shape[0] // arrays[3].shape[0]
    held = [pltpu.VMEM(s, a.dtype) for s, a in zip(held_shapes(n, arrays), arrays)]
    guest_blocks = held[7].shape[0] - n // 2
    guest_rows, guest_width = held[9].shape[1:]
    guests = [
        pltpu.VMEM((guest_blocks, guest_rows, guest_width), jnp.bfloat16),
        pltpu.VMEM((guest_blocks, guest_rows, guest_width + LANES), jnp.bfloat16),
        pltpu.VMEM((guest_blocks, guest_rows, guest_width + LANES), jnp.bfloat16),
    ]
    results = [
        pltpu.VMEM((n, *held[0].shape[1:]), jnp.bfloat16),
        pltpu.VMEM((n, *held[3].shape[1:]), jnp.bfloat16),
        pltpu.VMEM((n // 2, *held[6].shape[1:]), jnp.bfloat16),
        pltpu.VMEM((n // 2, *held[9].shape[1:]), jnp.bfloat16),
    ]
    shapes = [arrays[at].shape for at in (0, 3, 6, 9)]
    anywhere = pl.BlockSpec(memory_space=pl.ANY)
    scalars = pl.BlockSpec(memory_space=pltpu.SMEM)
    vectors = pl.BlockSpec(memory_space=pltpu.VMEM)
    mixed = pl.pallas_call(
        functools.partial(fused_kernel, n, ratio),
        out_shape=tuple(pltpu.VMEM(shape, jnp.bfloat16) for shape in shapes),
        in_specs=[scalars] * 3 + [pl.BlockSpec(memory_space=pltpu.HBM)] * 12,
        out_specs=(vectors,) * 4,
        scratch_shapes=held
        + results
        + [
            pltpu.SemaphoreType.DMA((12,)),
            pltpu.SemaphoreType.DMA((12,)),
            pltpu.SemaphoreType.DMA((15,)),
            pltpu.SemaphoreType.DMA((4,)),
            pltpu.SemaphoreType.DMA((4,)),
            pltpu.SemaphoreType.REGULAR((6,)),
            pltpu.SemaphoreType.DMA((2,)),
            *guests,
        ],
        compiler_params=pltpu.CompilerParams(
            collective_id=0, has_side_effects=True, vmem_limit_bytes=24 * 2**20
        ),
    )(*lengths, *arrays)
    return pl.pallas_call(
        write_out,
        out_shape=tuple(jax.ShapeDtypeStruct(shape, jnp.bfloat16) for shape in shapes),
        in_specs=[vectors] * 4,
        out_specs=(anywhere,) * 4,
        scratch_shapes=[pltpu.SemaphoreType.DMA((4,))],
        compiler_params=pltpu.CompilerParams(vmem_limit_bytes=2**20),
    )(*mixed)


def kernel_fits(n, video_rows, audio_rows):
    if n % 16 or HV % n or HA % n or (HV // n * HDV) % LANES or (HA // n * HDA) % LANES:
        return False
    ratio = video_rows // audio_rows
    return video_rows == ratio * audio_rows and ratio & (ratio - 1) == 0 and n * audio_rows % 16 == 0 and audio_rows % 8 == 0


def dispatch(*arguments):
    fits = kernel_fits(lax.axis_size("seq"), arguments[0].shape[0], arguments[3].shape[0])
    return (fused_shards if fits else shards)(*arguments)


def solution(mesh):
    placed = (
        P(("clip", "seq"), None),
        P(("clip", "seq"), None),
        P(("clip", "seq"), None),
        P(("clip", "seq"), None),
        P(("clip", "seq"), None),
        P(("clip", "seq"), None),
        P(("clip", "seq"), None),
        P(("clip", "seq"), None),
        P(("clip", "seq"), None),
        P(("clip", "seq"), None),
        P(("clip", "seq"), None),
        P(("clip", "seq"), None),
        P("clip"),
        P("clip"),
        P("clip"),
    )
    return jax.shard_map(
        dispatch,
        mesh=mesh,
        in_specs=placed,
        out_specs=(
            P(("clip", "seq"), None),
            P(("clip", "seq"), None),
            P(("clip", "seq"), None),
            P(("clip", "seq"), None),
        ),
        check_vma=False,
    )
```

```python
import contextlib
import functools
import math

import jax
import jax.numpy as jnp
from jax import lax
from jax.experimental import pallas as pl
from jax.experimental.pallas import tpu as pltpu
from jax.sharding import PartitionSpec as P

HV = 32
HDV = 128
HA = 32
HDA = 64


def block_size(total, limit):
    chosen = min(total, limit)
    while total % chosen:
        chosen -= 1
    return chosen


def split_heads(tokens, heads, depth, copies):
    rows = tokens.shape[0]
    shaped = tokens.reshape(copies, rows // copies, heads, depth).transpose(2, 0, 1, 3)
    return shaped.reshape(heads * copies, rows // copies, depth)


def spread_heads(tokens, heads, depth, copies):
    rows = tokens.shape[0]
    shaped = tokens.reshape(rows, heads, depth).transpose(1, 0, 2)
    shaped = jnp.broadcast_to(shaped[:, None], (heads, copies, rows, depth))
    return shaped.reshape(heads * copies, rows, depth)


def join_heads(owned, heads, depth, copies):
    part_rows = owned.shape[1]
    shaped = owned.reshape(heads, copies, part_rows, depth).transpose(1, 2, 0, 3)
    return shaped.reshape(copies * part_rows, heads * depth)


def owned_positions(rows, copies, devices, index):
    part_rows = rows // copies
    flat = jnp.arange(devices * part_rows, dtype=jnp.int32)
    return flat // part_rows * rows + index % copies * part_rows + flat % part_rows


def online_update(carry, scores, permit, value_tile, value_form):
    running, total, accum = carry
    scores = jnp.where(permit, scores, -1e30)
    newmax = jnp.maximum(running, jnp.max(scores, axis=2))
    weights = jnp.where(permit, jnp.exp(scores - newmax[:, :, None]), 0.0)
    factor = jnp.exp(running - newmax)
    total = total * factor + jnp.sum(weights, axis=2)
    mixed = jnp.einsum(
        value_form, weights.astype(jnp.bfloat16), value_tile, preferred_element_type=jnp.float32
    )
    accum = accum * factor[:, :, None] + mixed
    return (newmax, total, accum)


def fold_initial(rows, heads, depth):
    return (
        jnp.full((heads, rows), -1e30, jnp.float32),
        jnp.zeros((heads, rows), jnp.float32),
        jnp.zeros((heads, rows, depth), jnp.float32),
    )


def fold_piece(carry, local_query, key_rows, value_rows, permit, heads, depth):
    keyed = key_rows.reshape(key_rows.shape[0], heads, depth)
    valued = value_rows.reshape(value_rows.shape[0], heads, depth)
    scores = jnp.einsum("qhd,khd->hqk", local_query, keyed, preferred_element_type=jnp.float32) * (
        1.0 / math.sqrt(depth)
    )
    return online_update(carry, scores, permit[None], valued, "hqk,khd->hqd")


def fold_finish(carry, heads, depth):
    running, total, accum = carry
    result = (accum / total[:, :, None]).astype(jnp.bfloat16)
    return result.transpose(1, 0, 2).reshape(result.shape[1], heads * depth)


def attend_local(queries, keys, values, query_pos, key_pos, allowed):
    heads, q_count, depth = queries.shape
    k_count = keys.shape[1]
    q_block = block_size(q_count, 512)
    k_block = block_size(k_count, 2048)
    scale = 1.0 / math.sqrt(depth)
    q_tiles = queries.reshape(heads, q_count // q_block, q_block, depth).transpose(1, 0, 2, 3)
    k_tiles = keys.reshape(heads, k_count // k_block, k_block, depth).transpose(1, 0, 2, 3)
    v_tiles = values.reshape(heads, k_count // k_block, k_block, depth).transpose(1, 0, 2, 3)
    q_places = query_pos.reshape(q_count // q_block, q_block)
    k_places = key_pos.reshape(k_count // k_block, k_block)

    def one_tile(packed):
        q_tile, q_where = packed

        def absorb(carry, piece):
            k_tile, v_tile, k_where = piece
            scores = (
                jnp.einsum("hqd,hkd->hqk", q_tile, k_tile, preferred_element_type=jnp.float32)
                * scale
            )
            permit = allowed(q_where[:, None], k_where[None, :])[None]
            return (online_update(carry, scores, permit, v_tile, "hqk,hkd->hqd"), None)

        initial = fold_initial(q_block, heads, depth)
        final_state, unused = lax.scan(absorb, initial, (k_tiles, v_tiles, k_places))
        running, total, accum = final_state
        return (accum / total[:, :, None]).astype(jnp.bfloat16)

    tiles = lax.map(one_tile, (q_tiles, q_places))
    return tiles.transpose(1, 0, 2, 3).reshape(heads, q_count, depth)


def shards(
    video_query,
    video_keys,
    video_values,
    audio_query,
    audio_keys,
    audio_values,
    cross_video_query,
    cross_video_keys,
    cross_video_values,
    cross_audio_query,
    cross_audio_keys,
    cross_audio_values,
    video_length,
    audio_length,
    align_offset,
):
    devices = lax.axis_size("seq")
    index = lax.axis_index("seq")
    video_rows = video_query.shape[0]
    audio_rows = audio_query.shape[0]
    video_total = video_rows * devices
    audio_total = audio_rows * devices
    video_reach = video_total // 8
    audio_reach = 5 * audio_total // 8
    video_valid = video_length[0]
    audio_valid = audio_length[0]
    align_shift = align_offset[0]
    copies = max(devices // HV, 1)
    video_places = jnp.arange(video_total, dtype=jnp.int32)
    audio_places = jnp.arange(audio_total, dtype=jnp.int32)

    def video_open(q_where, k_where):
        return k_where < video_valid

    def toward_video(q_where, k_where):
        center = jnp.clip(q_where * audio_total // video_total + align_shift, 0, audio_valid - 1)
        return (k_where < audio_valid) & (jnp.abs(k_where - center) <= audio_reach)

    def toward_audio(q_where, k_where):
        center = jnp.clip((q_where - align_shift) * video_total // audio_total, 0, video_valid - 1)
        return (k_where < video_valid) & (jnp.abs(k_where - center) <= video_reach)

    video_owned = (
        lax.all_to_all(
            split_heads(video_query, HV, HDV, copies),
            "seq",
            split_axis=0,
            concat_axis=1,
            tiled=True,
        ),
        lax.all_to_all(
            spread_heads(video_keys, HV, HDV, copies),
            "seq",
            split_axis=0,
            concat_axis=1,
            tiled=True,
        ),
        lax.all_to_all(
            spread_heads(video_values, HV, HDV, copies),
            "seq",
            split_axis=0,
            concat_axis=1,
            tiled=True,
        ),
    )
    video_done = attend_local(
        video_owned[0],
        video_owned[1],
        video_owned[2],
        owned_positions(video_rows, copies, devices, index),
        video_places,
        video_open,
    )
    video_mixed = join_heads(
        lax.all_to_all(video_done, "seq", split_axis=1, concat_axis=0, tiled=True), HV, HDV, copies
    )
    audio_local = audio_query.reshape(audio_rows, HA, HDA)
    piece = (
        lax.all_gather(audio_keys, "seq", axis=0, tiled=True),
        lax.all_gather(audio_values, "seq", axis=0, tiled=True),
    )
    k_where = jnp.arange(piece[0].shape[0], dtype=jnp.int32)
    audio_k_where = k_where[None, :]
    permit = audio_k_where < audio_valid
    audio_state = fold_piece(
        fold_initial(audio_rows, HA, HDA), audio_local, piece[0], piece[1], permit, HA, HDA
    )
    audio_mixed = fold_finish(audio_state, HA, HDA)
    cross_owned = (
        lax.all_to_all(
            split_heads(cross_video_query, HA, HDA, copies),
            "seq",
            split_axis=0,
            concat_axis=1,
            tiled=True,
        ),
        lax.all_to_all(
            spread_heads(cross_audio_keys, HA, HDA, copies),
            "seq",
            split_axis=0,
            concat_axis=1,
            tiled=True,
        ),
        lax.all_to_all(
            spread_heads(cross_audio_values, HA, HDA, copies),
            "seq",
            split_axis=0,
            concat_axis=1,
            tiled=True,
        ),
    )
    cross_done = attend_local(
        cross_owned[0],
        cross_owned[1],
        cross_owned[2],
        owned_positions(video_rows, copies, devices, index),
        audio_places,
        toward_video,
    )
    video_cross = join_heads(
        lax.all_to_all(cross_done, "seq", split_axis=1, concat_axis=0, tiled=True), HA, HDA, copies
    )
    listen_owned = (
        lax.all_to_all(
            split_heads(cross_audio_query, HA, HDA, copies),
            "seq",
            split_axis=0,
            concat_axis=1,
            tiled=True,
        ),
        lax.all_to_all(
            spread_heads(cross_video_keys, HA, HDA, copies),
            "seq",
            split_axis=0,
            concat_axis=1,
            tiled=True,
        ),
        lax.all_to_all(
            spread_heads(cross_video_values, HA, HDA, copies),
            "seq",
            split_axis=0,
            concat_axis=1,
            tiled=True,
        ),
    )
    listen_done = attend_local(
        listen_owned[0],
        listen_owned[1],
        listen_owned[2],
        owned_positions(audio_rows, copies, devices, index),
        video_places,
        toward_audio,
    )
    audio_cross = join_heads(
        lax.all_to_all(listen_done, "seq", split_axis=1, concat_axis=0, tiled=True), HA, HDA, copies
    )
    return (video_mixed, audio_mixed, video_cross, audio_cross)


LANES = 128
mark = lambda name: contextlib.nullcontext()
KEYED = (7, 8)
PARTIAL = 3

GROUPS = (
    ((0, 1, 2), 0, False),
    ((3, 4, 5), 1, False),
    ((6, 10, 11), 2, True),
    ((9, 7, 8), 3, True),
)


def softmax_mix(query, keys, values, permit, scale):
    scores = lax.dot_general(
        query, keys, (((1,), (1,)), ((), ())), preferred_element_type=jnp.float32
    )
    scores = jnp.where(permit, scores * scale, -1e30)
    peak = jnp.max(scores, axis=1, keepdims=True)
    weights = jnp.exp(scores - peak)
    total = jnp.sum(weights, axis=1, keepdims=True)
    mixed = jnp.dot(weights.astype(jnp.bfloat16), values, preferred_element_type=jnp.float32)
    return mixed / total


def read_tokens(ref, column):
    block = ref[:, :, column : column + LANES]
    n, rows, _ = block.shape
    if rows % 16:
        return block.astype(jnp.float32).reshape(n * rows, LANES).astype(block.dtype)
    return block.reshape(n * rows, LANES)


def write_tokens(ref, column, result):
    n, rows, _ = ref.shape
    ref[:, :, column : column + LANES] = result.reshape(n, rows, LANES).astype(ref.dtype)


def margin_blocks(n, video_rows):
    return min(-(-(3 * n * video_rows // 16) // video_rows), n // 2)


def held_shapes(n, arrays):
    half = n // 2
    shapes = [None] * 12
    for group, which, halved in GROUPS:
        for place, at in enumerate(group):
            rows, cols = arrays[at].shape
            blocks = n
            if halved and place == 0:
                blocks = half
            elif which == 3:
                blocks = half + margin_blocks(n, rows)
            shapes[at] = (blocks, rows, cols // (half if halved else n))
    return shapes


def fused_kernel(n, ratio, *refs):
    video_length, audio_length, align_offset = refs[:3]
    arrays = refs[3:15]
    outs = refs[15:19]
    held = refs[19:31]
    results = refs[31:35]
    send_sem, far_sem, recv_sem, back_send, back_recv, stage_sem, part_sem, guest, part_out, part_in = refs[
        35:
    ]
    half = n // 2
    quarter = n // 4
    margin = held[7].shape[0] - half
    me = lax.axis_index("seq")
    side = me // half
    inner = lax.rem(me, half)
    near = (me >= half - margin) & (me < half + margin)
    lower = side == 0
    upper = side == 1
    hosted = near & lower
    edge_key = near & upper

    def arrival(at, same):
        if at in KEYED and same:
            return recv_sem.at[jnp.where(edge_key, 12 + KEYED.index(at), at)]
        return recv_sem.at[at]

    def columns(width, owner):
        return pl.ds(pl.multiple_of(owner * width, LANES), width)

    def slot_of(group, which, halved, at, to_side):
        if halved and at == group[0]:
            return inner
        if which == 3:
            return me - to_side * (half - margin)
        return me

    def send(at, owner, slot, peer, sem, same):
        pltpu.make_async_remote_copy(
            src_ref=arrays[at].at[:, columns(held[at].shape[2], owner)],
            dst_ref=held[at].at[slot],
            send_sem=sem.at[at],
            recv_sem=arrival(at, same),
            device_id={"seq": peer},
            device_id_type=pl.DeviceIdType.MESH,
        ).start()

    for group, which, halved in GROUPS:
        for at in group:
            pltpu.make_async_copy(
                arrays[at].at[:, columns(held[at].shape[2], inner if halved else me)],
                held[at].at[slot_of(group, which, halved, at, side)],
                arrival(at, True),
            ).start()

    col = quarter // 2
    level = me // quarter
    rank = lax.rem(me, quarter)
    core = lax.rem(rank, col)
    mine_col = rank - core
    next_col = col - mine_col
    central = (level == 1) | (level == 2)
    here = level * quarter
    sibling = (level + 1 - 2 * lax.rem(level, 2)) * quarter
    far_center = (2 - side) * quarter
    far_edge = (3 - 3 * side) * quarter

    barrier = pltpu.get_barrier_semaphore()

    def signal(sem, peer):
        pl.semaphore_signal(
            sem, inc=1, device_id={"seq": peer}, device_id_type=pl.DeviceIdType.MESH
        )

    def greet(base, first):
        @pl.loop(first, col)
        def _(step):
            signal(barrier, base + lax.rem(core + step, col))

    @pl.when(central)
    def _():
        greet(far_center + mine_col, 0)

    greet(here + mine_col, 1)

    @pl.when(central)
    def _():
        greet(here + next_col, 0)
        greet(sibling + mine_col, 0)

    with mark("BAR"):
        pl.semaphore_wait(barrier, jnp.where(central, 3 * col - 1, 2 * col - 1))

    def send_part(number, base, count, first, same):
        group, which, halved = GROUPS[number]
        spot = core if count == col else rank

        def sends():
            @pl.loop(first, count)
            def _(step):
                peer = base + lax.rem(spot + step, count)
                owner = lax.rem(peer, half) if halved else peer
                for at in group:
                    if halved and at == group[0] and not same:
                        continue
                    slot = slot_of(group, which, halved, at, side if same else 1 - side)
                    send(at, owner, slot, peer, send_sem if same else far_sem, same)

        if which == 3 and not same:
            pl.when(hosted)(sends)
        else:
            sends()

    def f(number):
        send_part(number, far_edge, quarter, 0, False)
        send_part(number, far_center, quarter, 0, False)

    def k(number):
        send_part(number, far_center, quarter, 0, False)

    def g(number):
        send_part(number, far_edge, quarter, 0, False)

    def s(number):
        send_part(number, sibling, quarter, 0, True)

    def v(number):
        group = GROUPS[number][0]

        @pl.when(hosted)
        def _():
            @pl.loop(0, half)
            def _(step):
                owner = lax.rem(inner + step, half)
                pltpu.make_async_remote_copy(
                    src_ref=arrays[group[0]].at[:, columns(held[group[0]].shape[2], owner)],
                    dst_ref=guest.at[me - (half - margin)],
                    send_sem=far_sem.at[group[0]],
                    recv_sem=recv_sem.at[14],
                    device_id={"seq": half + owner},
                    device_id_type=pl.DeviceIdType.MESH,
                ).start()

    def h(number):
        send_part(number, here, quarter, 1, True)

    across = rank + next_col - mine_col

    @pl.when(central & lower)
    def _():
        signal(stage_sem.at[0], here + across)
        send_part(0, far_center + mine_col, col, 0, False)
        h(0)
        with mark("Y"):
            pl.semaphore_wait(stage_sem.at[0], 1)
        send_part(0, far_center + next_col, col, 0, False)
        with mark("O"):
            pl.semaphore_wait(stage_sem.at[2], 1)
        signal(stage_sem.at[1], sibling + rank)
        signal(stage_sem.at[5], here + across)
        with mark("Y2"):
            pl.semaphore_wait(stage_sem.at[5], 1)
        signal(stage_sem.at[3], far_center + rank)
        s(0)
        with mark("B"):
            pl.semaphore_wait(stage_sem.at[3], 1)
        signal(stage_sem.at[4], sibling + rank)
        g(0)
        v(3)
        g(1)
        k(1)
        g(3)
        k(3)
        g(2)
        k(2)
        h(1)
        h(3)
        s(3)
        s(1)
        h(2)
        s(2)

    @pl.when(central & upper)
    def _():
        signal(stage_sem.at[0], here + across)
        send_part(0, far_center + mine_col, col, 0, False)
        h(0)
        with mark("Y"):
            pl.semaphore_wait(stage_sem.at[0], 1)
        send_part(0, far_center + next_col, col, 0, False)
        with mark("O"):
            pl.semaphore_wait(stage_sem.at[2], 1)
        signal(stage_sem.at[1], sibling + rank)
        signal(stage_sem.at[5], here + across)
        with mark("Y2"):
            pl.semaphore_wait(stage_sem.at[5], 1)
        signal(stage_sem.at[3], far_center + rank)
        s(0)
        with mark("B"):
            pl.semaphore_wait(stage_sem.at[3], 1)
        signal(stage_sem.at[4], sibling + rank)
        g(0)
        g(1)
        h(1)
        k(1)
        g(2)
        k(2)
        h(3)
        s(3)
        s(1)
        h(2)
        s(2)

    @pl.when(jnp.logical_not(central) & lower)
    def _():
        signal(stage_sem.at[2], sibling + rank)
        send_part(0, sibling + mine_col, col, 0, True)
        send_part(0, here + mine_col, col, 1, True)
        with mark("A"):
            pl.semaphore_wait(stage_sem.at[1], 1)
        k(0)
        send_part(0, sibling + next_col, col, 0, True)
        with mark("C"):
            pl.semaphore_wait(stage_sem.at[4], 1)
        g(0)
        send_part(0, here + next_col, col, 0, True)
        s(3)
        g(1)
        k(1)
        s(1)
        k(2)
        g(2)
        s(2)
        h(3)
        h(1)
        h(2)

    @pl.when(jnp.logical_not(central) & upper)
    def _():
        send_part(0, here + mine_col, col, 1, True)
        signal(stage_sem.at[2], sibling + rank)
        send_part(0, sibling + mine_col, col, 0, True)
        with mark("A"):
            pl.semaphore_wait(stage_sem.at[1], 1)
        k(0)
        send_part(0, sibling + next_col, col, 0, True)
        with mark("C"):
            pl.semaphore_wait(stage_sem.at[4], 1)
        g(0)
        send_part(0, here + next_col, col, 0, True)
        s(3)
        g(1)
        k(1)
        s(1)
        g(2)
        s(2)
        h(3)
        k(2)
        h(1)
        h(2)

    video_valid = video_length[0]
    audio_valid = audio_length[0]
    shift = align_offset[0]
    video_rows = arrays[0].shape[0]
    audio_rows = arrays[3].shape[0]
    video_total = n * video_rows
    audio_total = n * audio_rows
    video_reach = video_total // 8
    audio_reach = 5 * audio_total // 8

    def query_places(count, copies, first):
        rows = first + lax.broadcasted_iota(jnp.int32, (count, 1), 0)
        return jnp.concatenate([rows] * copies, axis=0)

    def key_places(count):
        return lax.broadcasted_iota(jnp.int32, (1, count), 1)

    def permit_of(which, copies):
        if which == 0:
            return key_places(video_total) < video_valid
        if which == 1:
            return key_places(audio_total) < audio_valid
        if which == 2:
            where = key_places(audio_total)
            spots = query_places(half * video_rows, copies, side * half * video_rows)
            spots = lax.shift_right_logical(spots, ratio.bit_length() - 1)
            center = jnp.clip(spots + shift, 0, audio_valid - 1)
            return (where < audio_valid) & (jnp.abs(where - center) <= audio_reach)
        return reach_permit(copies, side * half * audio_rows, half * audio_rows, side * (half - margin) * video_rows, (half + margin) * video_rows)

    def reach_permit(copies, query_first, query_count, key_first, key_count):
        where = key_places(key_count) + key_first
        spots = query_places(query_count, copies, query_first)
        center = jnp.clip((spots - shift) * ratio, 0, video_valid - 1)
        return (where < video_valid) & (jnp.abs(where - center) <= video_reach)

    def spread(tokens):
        lane = lax.broadcasted_iota(jnp.int32, tokens.shape, 1) // HDA
        zero = jnp.zeros_like(tokens)
        return jnp.concatenate(
            [jnp.where(lane == head, tokens, zero) for head in range(LANES // HDA)], axis=0
        )

    def fold(stacked):
        rows = stacked.shape[0] // (LANES // HDA)
        merged = jnp.broadcast_to(stacked[:rows], (rows, LANES))
        lane = lax.broadcasted_iota(jnp.int32, merged.shape, 1) // HDA
        for head in range(1, LANES // HDA):
            merged = jnp.where(lane == head, stacked[head * rows : (head + 1) * rows], merged)
        return merged

    def scored(tokens, keys, permit):
        scores = lax.dot_general(
            tokens, keys, (((1,), (1,)), ((), ())), preferred_element_type=jnp.float32
        )
        return jnp.where(permit, scores * (1.0 / math.sqrt(HDA)), -1e30)

    def weighed(scores, peak, permit, values):
        weights = jnp.where(permit, jnp.exp(scores - peak), 0.0)
        total = jnp.sum(weights, axis=1, keepdims=True)
        mixed = jnp.dot(weights.astype(jnp.bfloat16), values, preferred_element_type=jnp.float32)
        return mixed, total

    def tokens_of(ref, first, count, column):
        block = ref[first : first + count, :, column : column + LANES]
        rows = block.shape[1]
        if rows % 16:
            return block.astype(jnp.float32).reshape(count * rows, LANES).astype(block.dtype)
        return block.reshape(count * rows, LANES)

    group3 = GROUPS[3][0]
    heads_each = LANES // HDA

    def host_guests():
        copies = heads_each
        permit = reach_permit(
            copies,
            (half - margin) * audio_rows,
            margin * audio_rows,
            half * video_rows,
            margin * video_rows,
        )
        with mark("WG"):
            pltpu.make_async_copy(guest, guest, recv_sem.at[14]).wait()
            for at in KEYED:
                part = held[at].at[pl.ds(0, margin)]
                pltpu.make_async_copy(part, part, recv_sem.at[12 + KEYED.index(at)]).wait()
        keys, values = held[group3[1]], held[group3[2]]
        rows = margin * audio_rows
        lane = lax.broadcasted_iota(jnp.int32, (rows, LANES), 1)
        packed = jnp.zeros((rows, LANES), jnp.float32)
        for column in range(0, guest.shape[2], LANES):
            tokens = spread(tokens_of(guest, 0, margin, column))
            scores = scored(tokens, tokens_of(keys, margin, margin, column), permit)
            peak = jnp.max(scores, axis=1, keepdims=True).astype(jnp.bfloat16).astype(jnp.float32)
            mixed, total = weighed(scores, peak, permit, tokens_of(values, margin, margin, column))
            coarse = total.astype(jnp.bfloat16).astype(jnp.float32)
            for head in range(copies):
                spot = column // LANES * copies + head
                piece = slice(head * rows, (head + 1) * rows)
                for kind, stat in enumerate((peak, coarse, total - coarse)):
                    packed = jnp.where(lane == 3 * spot + kind, stat[piece], packed)
            part_out[:, :, column : column + LANES] = (
                fold(mixed).reshape(margin, audio_rows, LANES).astype(part_out.dtype)
            )
        part_out[:, :, guest.shape[2] :] = packed.reshape(margin, audio_rows, LANES).astype(
            part_out.dtype
        )
        pltpu.make_async_remote_copy(
            src_ref=part_out,
            dst_ref=part_in,
            send_sem=part_sem.at[0],
            recv_sem=part_sem.at[1],
            device_id={"seq": inner},
            device_id_type=pl.DeviceIdType.MESH,
        ).start()

    def wait_reach():
        for at in group3:
            with mark("W3_%d" % at):
                part = held[at].at[pl.ds(0, half)]
                pltpu.make_async_copy(part, part, recv_sem.at[at]).wait()

    def lower_reach():
        copies = heads_each
        permit = reach_permit(copies, 0, half * audio_rows, 0, half * video_rows)
        wait_reach()
        query, keys, values = (held[at] for at in group3)
        own = []
        for column in range(0, query.shape[2], LANES):
            tokens = spread(tokens_of(query, 0, half, column))
            scores = scored(tokens, tokens_of(keys, 0, half, column), permit)
            peak = jnp.max(scores, axis=1, keepdims=True)
            mixed, total = weighed(scores, peak, permit, tokens_of(values, 0, half, column))
            own.append((fold(mixed), fold(peak), fold(total)))
        return own

    def lower_join(own):
        copies = heads_each
        with mark("WP"):
            pltpu.make_async_copy(part_in, part_in, part_sem.at[1]).wait()
        first = (half - margin) * audio_rows
        rows = margin * audio_rows
        stats = part_in[:, :, guest.shape[2] :].astype(jnp.float32).reshape(rows, LANES)
        for index, (mixed, peak, total) in enumerate(own):
            column = index * LANES
            theirs = part_in[:, :, column : column + LANES].astype(jnp.float32).reshape(rows, LANES)

            def stat(kind):
                spots = [3 * (index * copies + head) + kind for head in range(copies)]
                return fold(jnp.concatenate([stats[:, spot : spot + 1] for spot in spots], axis=0))

            their_peak = stat(0)
            their_total = stat(1) + stat(2)
            top = jnp.maximum(peak[first:], their_peak)
            mine_factor = jnp.exp(peak[first:] - top)
            their_factor = jnp.exp(their_peak - top)
            joined = mixed[first:] * mine_factor + theirs * their_factor
            joined = joined / (total[first:] * mine_factor + their_total * their_factor)
            whole = jnp.concatenate([mixed[:first] / total[:first], joined], axis=0)
            write_tokens(results[3], column, whole)

    def upper_reach():
        copies = heads_each
        permit = permit_of(3, copies)
        wait_reach()
        query, keys, values = (held[at] for at in group3)
        for column in range(0, query.shape[2], LANES):
            tokens = spread(read_tokens(query, column))
            mixed = softmax_mix(
                tokens,
                read_tokens(keys, column),
                read_tokens(values, column),
                permit,
                1.0 / math.sqrt(HDA),
            )
            write_tokens(results[3], column, fold(mixed))

    def compute(number, low=None):
        group, which, halved = GROUPS[number]
        if which == 3:
            lower_join(lower_reach()) if low else upper_reach()
            return
        query, keys, values = (held[at] for at in group)
        depth = HDV if which == 0 else HDA
        copies = LANES // depth
        scale = 1.0 / math.sqrt(depth)
        permit = permit_of(which, copies)
        for at in group:
            with mark("W%d_%d" % (which, at)):
                pltpu.make_async_copy(held[at], held[at], recv_sem.at[at]).wait()
        for column in range(0, query.shape[2], LANES):
            tokens = read_tokens(query, column)
            if copies > 1:
                lane = lax.broadcasted_iota(jnp.int32, tokens.shape, 1) // depth
                zero = jnp.zeros_like(tokens)
                tokens = jnp.concatenate(
                    [jnp.where(lane == head, tokens, zero) for head in range(copies)], axis=0
                )
            mixed = softmax_mix(
                tokens, read_tokens(keys, column), read_tokens(values, column), permit, scale
            )
            if copies > 1:
                rows = mixed.shape[0] // copies
                merged = mixed[:rows]
                lane = lax.broadcasted_iota(jnp.int32, merged.shape, 1) // depth
                for head in range(1, copies):
                    merged = jnp.where(lane == head, mixed[head * rows : (head + 1) * rows], merged)
                mixed = merged
            write_tokens(results[which], column, mixed)

    def far_range(far):
        return {1: (0, half), 2: (0, col), 3: (col, half)}[int(far)]

    def give_back(number, far=False, close=False):
        group, which, halved = GROUPS[number]
        mine = inner if halved else me
        target = outs[which].at[:, columns(results[which].shape[2], mine)]

        def give(block, peer):
            pltpu.make_async_remote_copy(
                src_ref=results[which].at[block],
                dst_ref=target,
                send_sem=back_send.at[which],
                recv_sem=back_recv.at[which],
                device_id={"seq": peer},
                device_id_type=pl.DeviceIdType.MESH,
            ).start()

        if far:

            @pl.loop(*far_range(far))
            def _(step):
                peer = (1 - side) * half + step
                give(peer, peer)

        if not close:
            return

        @pl.loop(1, half)
        def _(step):
            block = jnp.where(step <= inner, step - 1, step)
            peer = side * half + block
            give(block if halved else peer, peer)

        pltpu.make_async_copy(results[which].at[mine], target, back_recv.at[which]).start()

    @pl.when(lower)
    def _():
        compute(0)
        own = lower_reach()
        give_back(0, close=True)
        compute(1)
        give_back(1, close=True)
        pl.when(central)(lambda: give_back(0, far=1))
        pl.when(central)(lambda: give_back(1, far=1))
        compute(2)
        give_back(2, far=False, close=True)
        pl.when(jnp.logical_not(central))(lambda: give_back(0, far=1))
        lower_join(own)
        give_back(3, far=False, close=True)
        pl.when(jnp.logical_not(central))(lambda: give_back(1, far=1))

    @pl.when(upper)
    def _():
        compute(0)
        give_back(0, close=True)
        pl.when(central)(lambda: give_back(0, far=3))
        pl.when(central)(lambda: give_back(0, far=2))
        host_guests()
        compute(1)
        give_back(1, close=True)
        pl.when(central)(lambda: give_back(1, far=2))
        pl.when(central)(lambda: give_back(1, far=3))
        pl.when(jnp.logical_not(central))(lambda: give_back(0, far=2))
        pl.when(jnp.logical_not(central))(lambda: give_back(1, far=2))
        pl.when(jnp.logical_not(central))(lambda: give_back(0, far=3))
        pl.when(jnp.logical_not(central))(lambda: give_back(1, far=3))
        compute(3, False)
        give_back(3, far=False, close=True)
        compute(2)
        give_back(2, far=False, close=True)


    def wait_bytes(ref, blocks, sem):
        part = ref.at[pl.ds(0, blocks)]
        pltpu.make_async_copy(part, part, sem).wait()

    for group, which, halved in GROUPS:
        for at in group:
            wait_bytes(held[at], half - 1, send_sem.at[at])
            if not halved or (which == 2 and at != group[0]):
                wait_bytes(held[at], half, far_sem.at[at])
            elif which == 3:

                @pl.when(hosted)
                def _(at=at):
                    wait_bytes(held[at], half, far_sem.at[at])

    @pl.when(upper)
    def _():
        pltpu.make_async_copy(part_out, part_out, part_sem.at[0]).wait()


    for which in range(4):
        wait_bytes(results[which], results[which].shape[0] - 1, back_send.at[which])

    for which in range(4):
        with mark("R%d" % which):
            pltpu.make_async_copy(outs[which], outs[which], back_recv.at[which]).wait()


def write_out(*refs):
    sources, targets, sem = refs[:4], refs[4:8], refs[8]
    copies = [pltpu.make_async_copy(*pair, sem.at[at]) for at, pair in enumerate(zip(sources, targets))]
    for copy in copies:
        copy.start()
    for copy in copies:
        copy.wait()


def fused_shards(*arguments):
    n = lax.axis_size("seq")
    arrays = arguments[:12]
    lengths = arguments[12:]
    arrays = [pltpu.with_memory_space_constraint(a, pltpu.HBM) for a in arrays]
    ratio = arrays[0].shape[0] // arrays[3].shape[0]
    held = [pltpu.VMEM(s, a.dtype) for s, a in zip(held_shapes(n, arrays), arrays)]
    guest_blocks = held[7].shape[0] - n // 2
    guest_rows, guest_width = held[9].shape[1:]
    guests = [
        pltpu.VMEM((guest_blocks, guest_rows, guest_width), jnp.bfloat16),
        pltpu.VMEM((guest_blocks, guest_rows, guest_width + LANES), jnp.bfloat16),
        pltpu.VMEM((guest_blocks, guest_rows, guest_width + LANES), jnp.bfloat16),
    ]
    results = [
        pltpu.VMEM((n, *held[0].shape[1:]), jnp.bfloat16),
        pltpu.VMEM((n, *held[3].shape[1:]), jnp.bfloat16),
        pltpu.VMEM((n // 2, *held[6].shape[1:]), jnp.bfloat16),
        pltpu.VMEM((n // 2, *held[9].shape[1:]), jnp.bfloat16),
    ]
    shapes = [arrays[at].shape for at in (0, 3, 6, 9)]
    anywhere = pl.BlockSpec(memory_space=pl.ANY)
    scalars = pl.BlockSpec(memory_space=pltpu.SMEM)
    vectors = pl.BlockSpec(memory_space=pltpu.VMEM)
    mixed = pl.pallas_call(
        functools.partial(fused_kernel, n, ratio),
        out_shape=tuple(pltpu.VMEM(shape, jnp.bfloat16) for shape in shapes),
        in_specs=[scalars] * 3 + [pl.BlockSpec(memory_space=pltpu.HBM)] * 12,
        out_specs=(vectors,) * 4,
        scratch_shapes=held
        + results
        + [
            pltpu.SemaphoreType.DMA((12,)),
            pltpu.SemaphoreType.DMA((12,)),
            pltpu.SemaphoreType.DMA((15,)),
            pltpu.SemaphoreType.DMA((4,)),
            pltpu.SemaphoreType.DMA((4,)),
            pltpu.SemaphoreType.REGULAR((6,)),
            pltpu.SemaphoreType.DMA((2,)),
            *guests,
        ],
        compiler_params=pltpu.CompilerParams(
            collective_id=0, has_side_effects=True, vmem_limit_bytes=24 * 2**20
        ),
    )(*lengths, *arrays)
    return pl.pallas_call(
        write_out,
        out_shape=tuple(jax.ShapeDtypeStruct(shape, jnp.bfloat16) for shape in shapes),
        in_specs=[vectors] * 4,
        out_specs=(anywhere,) * 4,
        scratch_shapes=[pltpu.SemaphoreType.DMA((4,))],
        compiler_params=pltpu.CompilerParams(vmem_limit_bytes=2**20),
    )(*mixed)


def kernel_fits(n, video_rows, audio_rows):
    if n % 16 or HV % n or HA % n or (HV // n * HDV) % LANES or (HA // n * HDA) % LANES:
        return False
    ratio = video_rows // audio_rows
    return video_rows == ratio * audio_rows and ratio & (ratio - 1) == 0 and n * audio_rows % 16 == 0 and audio_rows % 8 == 0


def dispatch(*arguments):
    fits = kernel_fits(lax.axis_size("seq"), arguments[0].shape[0], arguments[3].shape[0])
    return (fused_shards if fits else shards)(*arguments)


def solution(mesh):
    placed = (
        P(("clip", "seq"), None),
        P(("clip", "seq"), None),
        P(("clip", "seq"), None),
        P(("clip", "seq"), None),
        P(("clip", "seq"), None),
        P(("clip", "seq"), None),
        P(("clip", "seq"), None),
        P(("clip", "seq"), None),
        P(("clip", "seq"), None),
        P(("clip", "seq"), None),
        P(("clip", "seq"), None),
        P(("clip", "seq"), None),
        P("clip"),
        P("clip"),
        P("clip"),
    )
    return jax.shard_map(
        dispatch,
        mesh=mesh,
        in_specs=placed,
        out_specs=(
            P(("clip", "seq"), None),
            P(("clip", "seq"), None),
            P(("clip", "seq"), None),
            P(("clip", "seq"), None),
        ),
        check_vma=False,
    )
```
